512 devices in a mesh: seq: 32 (over x, z_lo), head: 16 (over y, z_hi, core).
Axes of the slice: x: 4, y: 4, z: 16 (z_hi: 2, z_lo: 8; z = z_hi * 8 + z_lo), core: 2. Of those that a mesh axis runs over, the one named last changes fastest.
Arguments:
- queries: bfloat16 [32, 16384, 128], P('head', 'seq'), may hold values from -30 to 30
- key_tokens: bfloat16 [16, 16384, 128], P('head', 'seq'), may hold values from -12 to 12
- value_tokens: bfloat16 [16, 16384, 128], P('head', 'seq'), may hold values from -6 to 6
- output_gradient: bfloat16 [32, 16384, 128], P('head', 'seq'), may hold values from -144 to 144
- summary_proj: bfloat16 [256, 16384], P(None, 'seq'), may hold values from -0.046875 to 0.046875
- partner_bits: int32 [32, 4], P('seq'), may hold values from 0 to 4, all different within a row
Outputs:
- attention_out: bfloat16 [32, 16384, 128], P('head', 'seq')
- query_grad: bfloat16 [32, 16384, 128], P('head', 'seq')
- key_grad: bfloat16 [16, 16384, 128], P('head', 'seq')
- value_grad: bfloat16 [16, 16384, 128], P('head', 'seq')
- proj_grad: float32 [256, 16384], P('head', 'seq')
The draws below stay inside these ranges and needn't reach their ends.
Inputs may be any that keep to these rules, and one draw needn't show every extreme that they name: `partner_bits`: each row names 4 different bit positions.
All inputs are finite; a program needn't handle non-finite values.
Results may differ from the reference program's by a relative error of at most 0.025.
Values may be sent and summed in bfloat16 or wider, within the bound.
A program may use at most 64 MiB of HBM per device.

```python
import math
import jax
import jax.numpy as jnp
from jax import lax

QUERY_HEADS = 32
KEY_VALUE_HEADS = 16
HEAD_SIZE = 128
BLOCK = 512
PARTNERS = 4
S_SUM = 256
BITS = 5
BLOCK_COUNT = 32
TOKEN_COUNT = 16384


def paired_draw(key):
    base_key = jax.random.fold_in(key, 7301)
    random_subkeys = jax.random.split(base_key, 4)
    queries = jax.random.truncated_normal(random_subkeys[0], -4.0, 4.0, (QUERY_HEADS, TOKEN_COUNT, HEAD_SIZE), jnp.float32)
    key_tokens = jax.random.truncated_normal(random_subkeys[1], -4.0, 4.0, (KEY_VALUE_HEADS, TOKEN_COUNT, HEAD_SIZE), jnp.float32)
    query_scale = jnp.exp(jax.random.uniform(random_subkeys[2], (QUERY_HEADS, TOKEN_COUNT, 1), jnp.float32, math.log(0.4), math.log(2.5)))
    key_factor_scale = jnp.exp(jax.random.uniform(random_subkeys[3], (KEY_VALUE_HEADS, TOKEN_COUNT, 1), jnp.float32, math.log(0.3), math.log(3.0)))
    queries = queries * query_scale
    key_tokens = key_tokens * key_factor_scale
    return (queries, key_tokens)


def draw_queries(key, part):
    return paired_draw(key)[0].astype(jnp.bfloat16)


def draw_key_tokens(key, part):
    return paired_draw(key)[1].astype(jnp.bfloat16)


def shard_levels(own_key, shape, shards, low, largest):
    def one(dim, blocks):
        draws = jax.random.uniform(jax.random.fold_in(jax.random.fold_in(own_key, 6), dim), (blocks,), jnp.float32, low / len(shards), largest / len(shards))
        return jnp.repeat(jnp.exp(draws), shape[dim] // blocks).reshape((-1,) + (1,) * (len(shape) - dim - 1))

    factor_of = one(*shards[0])
    for cut in shards[1:]:
        factor_of = factor_of * one(*cut)
    return factor_of


def distinct(rng, rows, number_of, top, lift):
    sequence = jax.random.permutation(jax.random.fold_in(rng, 1), number_of)
    boost = sequence
    for power in range(3):
        boost = boost * boost // number_of
    boost = boost * lift // number_of
    chance = jax.random.randint(jax.random.fold_in(rng, 2), (rows, number_of), 0, 4096) + boost
    holders = jax.random.permutation(jax.random.fold_in(rng, 3), rows)[jnp.arange(number_of) % rows]
    chance = jnp.where(jnp.arange(rows)[:, None] == holders[None, :], 1 << 14, chance)
    priority = chance * number_of + jnp.arange(number_of)
    return lax.top_k(priority.astype(jnp.int32), top)[1].astype(jnp.int32)


def gaussian(key, extent, width, bound, cuts=(), kind=jnp.bfloat16):
    array = jax.random.normal(key, extent, jnp.float32) * width
    if len(cuts) > 0:
        array = shard_levels(key, extent, cuts, -0.22, 0.18) * array
    return jnp.clip(array, min=-bound, max=bound).astype(kind)


def setup_inputs(seed: int = 0) -> dict:
    streams_of = jax.random.split(jax.random.key(seed), 7)
    return {
        "queries": draw_queries(jax.random.fold_in(streams_of[6], 71), 0),
        "key_tokens": draw_key_tokens(jax.random.fold_in(streams_of[6], 71), 0),
        "value_tokens": gaussian(streams_of[2], (KEY_VALUE_HEADS, TOKEN_COUNT, HEAD_SIZE), 1.0, 6.0, ((0, 16), (1, 32))),
        "output_gradient": gaussian(streams_of[3], (QUERY_HEADS, TOKEN_COUNT, HEAD_SIZE), 24.0, 144.0, ((0, 16), (1, 32))),
        "summary_proj": gaussian(streams_of[4], (S_SUM, TOKEN_COUNT), TOKEN_COUNT ** -0.5, 0.046875, ((1, 32),)),
        "partner_bits": distinct(streams_of[5], BLOCK_COUNT, BITS, PARTNERS, 0),
    }


score_scale = 1.0 / 12.0
highest = lax.Precision.HIGHEST


def rounded(tensor):
    return lax.optimization_barrier(tensor.astype(jnp.bfloat16)).astype(jnp.float32)


def block_pass(input_arrays):
    query_pair, grad_pair, key_set, value_set = input_arrays
    query_wide = query_pair.astype(jnp.float32)
    grad_wide = grad_pair.astype(jnp.float32)
    keys_wide = key_set.astype(jnp.float32)
    values_wide = value_set.astype(jnp.float32)
    scores = jnp.einsum("gqd,kd->gqk", query_wide, keys_wide, precision=highest) * score_scale
    row_max = jnp.max(scores, axis=-1, keepdims=True)
    exponent = jnp.exp(scores - row_max)
    row_total = jnp.sum(exponent, axis=-1, keepdims=True)
    attended = jnp.einsum("gqk,kd->gqd", rounded(exponent), values_wide, precision=highest) / row_total
    row_delta = jnp.sum(grad_wide * attended, axis=-1, keepdims=True)
    prob_grad = jnp.einsum("gqd,kd->gqk", grad_wide, values_wide, precision=highest)
    probabilities = exponent / row_total
    grad_scores = rounded(probabilities * (prob_grad - row_delta))
    weights_back = rounded(probabilities)
    query_grad = jnp.einsum("gqk,kd->gqd", grad_scores, keys_wide, precision=highest) * score_scale
    key_grads = jnp.einsum("gqk,gqd->kd", grad_scores, query_wide, precision=highest) * score_scale
    value_grads = jnp.einsum("gqk,gqd->kd", weights_back, grad_wide, precision=highest)
    return attended.astype(jnp.bfloat16), query_grad.astype(jnp.bfloat16), key_grads, value_grads


def reference(queries, key_tokens, value_tokens, output_gradient, summary_proj, partner_bits):
    group_width = QUERY_HEADS // KEY_VALUE_HEADS
    proj_wide = summary_proj.astype(jnp.float32)
    block_ids = jnp.arange(BLOCK_COUNT, dtype=jnp.int32)[:, None]
    partners = jnp.bitwise_xor(block_ids, jnp.left_shift(jnp.ones_like(partner_bits), partner_bits)).astype(jnp.int32)
    flat_partners = partners.reshape(BLOCK_COUNT * PARTNERS)
    split_at = (PARTNERS + 1) * BLOCK

    def sets_of(head_rows, summary_rows):
        blocks_here = head_rows.reshape(BLOCK_COUNT, BLOCK, HEAD_SIZE)
        joined = jnp.concatenate([blocks_here[:, None], blocks_here[partners]], axis=1)
        joined = joined.reshape(BLOCK_COUNT, split_at, HEAD_SIZE)
        tiled = jnp.broadcast_to(summary_rows[None], (BLOCK_COUNT, S_SUM, HEAD_SIZE))
        return jnp.concatenate([joined, tiled], axis=1)

    def finish(grads, head_wide):
        summary_grads = jnp.sum(grads[:, split_at:], axis=0)
        partner_rows = rounded(grads[:, BLOCK:split_at]).reshape(BLOCK_COUNT * PARTNERS, BLOCK, HEAD_SIZE)
        returned = jnp.zeros((BLOCK_COUNT, BLOCK, HEAD_SIZE), jnp.float32).at[flat_partners].add(partner_rows)
        through_summary = jnp.dot(proj_wide.T, summary_grads, precision=highest).reshape(BLOCK_COUNT, BLOCK, HEAD_SIZE)
        total_grad = grads[:, :BLOCK] + through_summary + returned
        proj_term = jnp.dot(summary_grads, head_wide.T, precision=highest)
        return total_grad.reshape(TOKEN_COUNT, HEAD_SIZE).astype(jnp.bfloat16), proj_term

    def head_pass(running, input_arrays):
        query_head, grad_head, key_head, value_head = input_arrays
        key_wide = key_head.astype(jnp.float32)
        value_wide = value_head.astype(jnp.float32)
        summary_keys = jnp.dot(proj_wide, key_wide, precision=highest).astype(jnp.bfloat16)
        summary_values = jnp.dot(proj_wide, value_wide, precision=highest).astype(jnp.bfloat16)
        key_sets = sets_of(key_head, summary_keys)
        value_sets = sets_of(value_head, summary_values)
        query_blocks = query_head.reshape(group_width, BLOCK_COUNT, BLOCK, HEAD_SIZE).transpose(1, 0, 2, 3)
        grad_blocks = grad_head.reshape(group_width, BLOCK_COUNT, BLOCK, HEAD_SIZE).transpose(1, 0, 2, 3)
        attended, query_grad, key_grads, value_grads = lax.map(block_pass, (query_blocks, grad_blocks, key_sets, value_sets))
        key_grad, key_term = finish(key_grads, key_wide)
        value_grad, value_term = finish(value_grads, value_wide)
        attended = attended.transpose(1, 0, 2, 3).reshape(group_width, TOKEN_COUNT, HEAD_SIZE)
        query_grad = query_grad.transpose(1, 0, 2, 3).reshape(group_width, TOKEN_COUNT, HEAD_SIZE)
        return running + key_term + value_term, (attended, query_grad, key_grad, value_grad)

    input_arrays = (queries.reshape(KEY_VALUE_HEADS, group_width, TOKEN_COUNT, HEAD_SIZE), output_gradient.reshape(KEY_VALUE_HEADS, group_width, TOKEN_COUNT, HEAD_SIZE), key_tokens, value_tokens)
    proj_grad, outputs = lax.scan(head_pass, jnp.zeros((S_SUM, TOKEN_COUNT), jnp.float32), input_arrays)
    attended, query_grad, key_grad, value_grad = outputs
    return attended.reshape(QUERY_HEADS, TOKEN_COUNT, HEAD_SIZE), query_grad.reshape(QUERY_HEADS, TOKEN_COUNT, HEAD_SIZE), key_grad, value_grad, proj_grad
```

```python
import functools
import math

import jax
import jax.numpy as jnp
from jax import lax
from jax.experimental import pallas as pl
from jax.experimental.pallas import tpu as pltpu
from jax.sharding import PartitionSpec as P

MESH = pl.DeviceIdType.MESH
BLOCK = 512
DIM = 128
ROWS = 1024
SUM = 256
CHUNK = 512
SCALE = 1.0 / 12.0
EXP2_SCALE = math.log2(math.e) / 12.0
F32, BF16 = jnp.float32, jnp.bfloat16

ORDER = (3, 0, 4, 1, 2)
Z_MASKS = tuple(range(1, 8))
X_MASKS = (8, 16, 24)
Y_MASKS = (4, 8, 12)

OWN, SLOT, SUMMARY = 0, 1, 5


def flipped(index, mask):
    out = index
    bit = 1
    while bit <= mask:
        if mask & bit:
            out = out + bit * (1 - 2 * lax.rem(lax.div(index, bit), 2))
        bit *= 2
    return out


def dot(a, b):
    return lax.dot_general(a, b, (((1,), (0,)), ((), ())), preferred_element_type=F32)


def dot_nt(a, b):
    return lax.dot_general(a, b, (((1,), (1,)), ((), ())), preferred_element_type=F32)


def dot_tn(a, b):
    return lax.dot_general(a, b, (((0,), (0,)), ((), ())), preferred_element_type=F32)


def kernel(
    bits_ref, q_ref, k_ref, v_ref, do_ref, proj_ref,
    out_ref, dq_ref, dk_ref, dv_ref, dproj_ref,
    qt, dot_t, part, rx, s8, rz, agz, agx,
    kr, vr, ks, vs, e_ref, m_ref, l_ref, mslot, acc, dqt,
    gka, gva, own_gk, own_gv, gslot_k, gslot_v, gk, gv, rgk, rgv,
    part2, rx2, s82, rz2, agz2, agx2,
    t_ref, rc, u_ref, ry, w_ref, rh,
    send_sem, recv_sem,
):
    seq = lax.axis_index("seq")
    head = lax.axis_index("head")
    my_x, my_z = lax.div(seq, 8), lax.rem(seq, 8)
    my_y, my_hi, my_core = lax.div(head, 4), lax.rem(lax.div(head, 2), 2), lax.rem(head, 2)

    barrier = pltpu.get_barrier_semaphore()
    peers = [("seq", m) for m in Z_MASKS + X_MASKS] + [("head", m) for m in (1, 2) + Y_MASKS]
    for axis, mask in peers:
        me = seq if axis == "seq" else head
        pl.semaphore_signal(barrier, inc=1, device_id={axis: flipped(me, mask)}, device_id_type=MESH)

    ids = iter(range(200))

    def copy(src, dst, axis, mask):
        me = seq if axis == "seq" else head
        n = next(ids)
        c = pltpu.make_async_remote_copy(
            src_ref=src, dst_ref=dst, send_sem=send_sem.at[n], recv_sem=recv_sem.at[n],
            device_id={axis: flipped(me, mask)}, device_id_type=MESH,
        )
        c.start()
        sent.append(c)
        return c

    sent = []

    proj = proj_ref[...]
    part[0:16] = dot(proj, k_ref[...]).reshape(16, 16, DIM)
    part[16:32] = dot(proj, v_ref[...]).reshape(16, 16, DIM)
    qt[...] = q_ref[...].T
    dot_t[...] = do_ref[...].T

    missing = 10 - (bits_ref[0, 0] + bits_ref[0, 1] + bits_ref[0, 2] + bits_ref[0, 3])
    place = jnp.int32(0)
    for i, b in enumerate(ORDER):
        place = place + jnp.where(missing == b, i, 0)

    pl.semaphore_wait(barrier, len(peers))

    def fetch(i):
        mask = 1 << ORDER[i]
        return (
            copy(k_ref, kr.at[i], "seq", mask),
            copy(v_ref, vr.at[i], "seq", mask),
        )

    def wait_recv(cs):
        for c in cs:
            c.wait_recv()

    def scatter_x(src, dst):
        return [
            copy(src.at[pl.ds(lax.div(flipped(seq, m), 8) * 8, 8)], dst.at[j], "seq", m)
            for j, m in enumerate(X_MASKS)
        ]

    def scatter_z(src, dst):
        return [
            copy(src.at[lax.rem(flipped(seq, m), 8)], dst.at[j], "seq", m)
            for j, m in enumerate(Z_MASKS)
        ]

    def gather_z(buf):
        return [copy(buf.at[my_z], buf.at[my_z], "seq", m) for m in Z_MASKS]

    def gather_x(src, dst):
        return [copy(src, dst.at[my_x], "seq", m) for m in X_MASKS]

    def forward(row, n, k, v, first=False):
        base = row * BLOCK

        def step(c, carry):
            cols = pl.ds(pl.multiple_of(c * CHUNK, CHUNK), CHUNK)
            s = dot(k[...], qt[:, cols])
            top = jnp.max(s, axis=0, keepdims=True)
            if not first:
                before = m_ref[:, cols]
                top = jnp.maximum(before, top)
                alpha = jnp.exp2((before - top) * EXP2_SCALE)
            e = jnp.exp2((s - top) * EXP2_SCALE)
            total = jnp.sum(e, axis=0, keepdims=True)
            eb = e.astype(BF16)
            e_ref[base : base + n, cols] = eb
            mixed = dot_tn(v[...], eb)
            if not first:
                total = l_ref[:, cols] * alpha + total
                mixed = acc[:, cols] * alpha + mixed
            l_ref[:, cols] = total
            acc[:, cols] = mixed
            m_ref[:, cols] = top
            mslot[row : row + 1, cols] = top
            return carry

        lax.fori_loop(0, ROWS // CHUNK, step, 0)

    def choose(i):
        early = i < place
        ks[i] = jnp.where(early, kr[i], kr[i + 1])
        vs[i] = jnp.where(early, vr[i], vr[i + 1])

    xs = scatter_x(part, rx)
    f_x1 = fetch(0)
    f_z1 = fetch(1)
    f_x2 = fetch(2)
    forward(OWN, BLOCK, k_ref, v_ref, first=True)
    wait_recv(xs)
    mine = part[pl.ds(my_x * 8, 8)]
    s8[...] = mine + rx[0] + rx[1] + rx[2]
    zs = scatter_z(s8, rz)
    f_z2 = fetch(3)
    wait_recv(f_x1 + f_z1)
    choose(0)
    forward(SLOT, BLOCK, ks.at[0], vs.at[0])
    wait_recv(zs)
    total = s8[my_z]
    for j in range(7):
        total = total + rz[j]
    agz[my_z] = total.astype(BF16)
    zg = gather_z(agz)
    f_z4 = fetch(4)
    wait_recv(f_x2)
    choose(1)
    forward(SLOT + 1, BLOCK, ks.at[1], vs.at[1])
    wait_recv(zg)
    xg = gather_x(agz, agx)
    agx[my_x] = agz[...]
    wait_recv(f_z2)
    choose(2)
    forward(SLOT + 2, BLOCK, ks.at[2], vs.at[2])
    wait_recv(xg)
    summary_k = agx[0:2].reshape(SUM, DIM)
    summary_v = agx[2:4].reshape(SUM, DIM)
    sk, sv = ks.at[4, 0:SUM], vs.at[4, 0:SUM]
    sk[...] = summary_k
    sv[...] = summary_v
    forward(SUMMARY, SUM, sk, sv)
    wait_recv(f_z4)
    choose(3)
    forward(SLOT + 3, BLOCK, ks.at[3], vs.at[3])

    inverse = 1.0 / l_ref[...]
    attended = acc[...] * inverse
    delta = jnp.sum(attended * dot_t[...].astype(F32), axis=0, keepdims=True)
    l_ref[...] = inverse
    acc[0:1, :] = delta
    out_ref[...] = attended.T.astype(BF16)
    dqt[...] = jnp.zeros_like(dqt)

    def backward(row, n, k, v, gk_acc, gv_acc):
        base = row * BLOCK
        gk_acc[...] = jnp.zeros_like(gk_acc)
        gv_acc[...] = jnp.zeros_like(gv_acc)

        def step(c, carry):
            cols = pl.ds(pl.multiple_of(c * CHUNK, CHUNK), CHUNK)
            factor = jnp.exp2((mslot[row : row + 1, cols] - m_ref[:, cols]) * EXP2_SCALE) * l_ref[:, cols]
            p = e_ref[base : base + n, cols].astype(F32) * factor
            dp = dot(v[...], dot_t[:, cols])
            ds = (p * (dp - acc[0:1, cols])).astype(BF16)
            dqt[:, cols] += dot_tn(k[...], ds)
            gk_acc[...] += dot(ds, q_ref[cols, :])
            gv_acc[...] += dot(p.astype(BF16), do_ref[cols, :])
            return carry

        lax.fori_loop(0, ROWS // CHUNK, step, 0)

    half_k, half_v = gka.at[0:SUM], gva.at[0:SUM]
    backward(SUMMARY, SUM, sk, sv, half_k, half_v)
    part2[0:16] = (half_k[...] * SCALE).astype(BF16).reshape(16, 16, DIM)
    part2[16:32] = half_v[...].astype(BF16).reshape(16, 16, DIM)
    xs = scatter_x(part2, rx2)

    def slot_back(i):
        backward(SLOT + i, BLOCK, ks.at[i], vs.at[i], gka, gva)
        gslot_k[i] = (gka[...] * SCALE).astype(BF16)
        gslot_v[i] = gva[...].astype(BF16)

    def give_back(i):
        for slots, g in ((gslot_k, gk), (gslot_v, gv)):
            zero = jnp.zeros((BLOCK, DIM), BF16)
            early = slots[i] if i < 4 else zero
            late = slots[i - 1] if i > 0 else zero
            g[i] = jnp.where(i < place, early, jnp.where(i > place, late, zero))
        mask = 1 << ORDER[i]
        return (
            copy(gk.at[i], rgk.at[i], "seq", mask),
            copy(gv.at[i], rgv.at[i], "seq", mask),
        )

    slot_back(3)
    wait_recv(xs)
    s82[...] = (
        part2[pl.ds(my_x * 8, 8)].astype(F32) + rx2[0].astype(F32) + rx2[1].astype(F32) + rx2[2].astype(F32)
    )
    zs = scatter_z(s82, rz2)
    slot_back(2)
    r_z2 = give_back(3)
    slot_back(1)
    wait_recv(zs)
    total = s82[my_z]
    for j in range(7):
        total = total + rz2[j]
    agz2[my_z] = total.astype(BF16)
    zg = gather_z(agz2)
    r_z4 = give_back(4)
    r_x2 = give_back(2)
    slot_back(0)
    r_z1 = give_back(1)
    r_x1 = give_back(0)
    wait_recv(zg)
    xg = gather_x(agz2, agx2)
    agx2[my_x] = agz2[...]
    backward(OWN, BLOCK, k_ref, v_ref, own_gk, own_gv)
    dq_ref[...] = (dqt[...] * SCALE).T.astype(BF16)
    wait_recv(xg)
    sg_k = agx2[0:2].reshape(SUM, DIM)
    sg_v = agx2[2:4].reshape(SUM, DIM)
    term = dot_nt(sg_k, k_ref[...]) + dot_nt(sg_v, v_ref[...])
    term = term.astype(BF16).reshape(8, 2, 16, BLOCK)
    t_ref[0] = term[:, 0]
    t_ref[1] = term[:, 1]
    c_core = copy(t_ref.at[1 - my_core], rc, "head", 1)
    own_gk[...] = own_gk[...] * SCALE + dot_tn(proj_ref[...], sg_k)
    own_gv[...] = own_gv[...] + dot_tn(proj_ref[...], sg_v)
    c_core.wait_recv()
    u_ref[...] = (t_ref[my_core].astype(F32) + rc[...].astype(F32)).astype(BF16).reshape(4, 2, 16, BLOCK)
    ys = [
        copy(u_ref.at[lax.div(flipped(head, m), 4)], ry.at[j], "head", m)
        for j, m in enumerate(Y_MASKS)
    ]
    wait_recv(ys)
    w_ref[...] = u_ref[my_y].astype(F32) + ry[0].astype(F32) + ry[1].astype(F32) + ry[2].astype(F32)
    hs = copy(w_ref.at[1 - my_hi], rh, "head", 2)
    for c, i in ((r_x1, 0), (r_x2, 2), (r_z1, 1), (r_z2, 3)):
        wait_recv(c)
        own_gk[...] += rgk[i].astype(F32)
        own_gv[...] += rgv[i].astype(F32)
    wait_recv(r_z4)
    dk_ref[...] = (own_gk[...] + rgk[4].astype(F32)).astype(BF16)
    dv_ref[...] = (own_gv[...] + rgv[4].astype(F32)).astype(BF16)
    hs.wait_recv()
    dproj_ref[...] = w_ref[my_hi] + rh[...]
    for c in sent:
        c.wait_send()


def per_device(queries, key_tokens, value_tokens, output_gradient, summary_proj, partner_bits):
    vmem = pl.BlockSpec(memory_space=pltpu.VMEM)
    smem = pl.BlockSpec(memory_space=pltpu.SMEM)
    V = pltpu.VMEM
    copies = 68
    out, dq, dk, dv, dproj = pl.pallas_call(
        kernel,
        name="butterfly",
        out_shape=(
            jax.ShapeDtypeStruct((ROWS, DIM), BF16),
            jax.ShapeDtypeStruct((ROWS, DIM), BF16),
            jax.ShapeDtypeStruct((BLOCK, DIM), BF16),
            jax.ShapeDtypeStruct((BLOCK, DIM), BF16),
            jax.ShapeDtypeStruct((16, BLOCK), F32),
        ),
        in_specs=[smem] + [vmem] * 5,
        out_specs=[vmem] * 5,
        scratch_shapes=[
            V((DIM, ROWS), BF16), V((DIM, ROWS), BF16),
            V((32, 16, DIM), F32), V((3, 8, 16, DIM), F32),
            V((8, 16, DIM), F32), V((7, 16, DIM), F32),
            V((8, 16, DIM), BF16), V((4, 8, 16, DIM), BF16),
            V((5, BLOCK, DIM), BF16), V((5, BLOCK, DIM), BF16),
            V((5, BLOCK, DIM), BF16), V((5, BLOCK, DIM), BF16),
            V((5 * BLOCK + SUM, ROWS), BF16),
            V((1, ROWS), F32), V((1, ROWS), F32), V((8, ROWS), F32),
            V((DIM, ROWS), F32), V((DIM, ROWS), F32),
            V((BLOCK, DIM), F32), V((BLOCK, DIM), F32),
            V((BLOCK, DIM), F32), V((BLOCK, DIM), F32),
            V((4, BLOCK, DIM), BF16), V((4, BLOCK, DIM), BF16),
            V((5, BLOCK, DIM), BF16), V((5, BLOCK, DIM), BF16),
            V((5, BLOCK, DIM), BF16), V((5, BLOCK, DIM), BF16),
            V((32, 16, DIM), BF16), V((3, 8, 16, DIM), BF16),
            V((8, 16, DIM), F32), V((7, 16, DIM), F32),
            V((8, 16, DIM), BF16), V((4, 8, 16, DIM), BF16),
            V((2, 8, 16, BLOCK), BF16), V((8, 16, BLOCK), BF16),
            V((4, 2, 16, BLOCK), BF16), V((3, 2, 16, BLOCK), BF16),
            V((2, 16, BLOCK), F32), V((16, BLOCK), F32),
            pltpu.SemaphoreType.DMA((copies,)), pltpu.SemaphoreType.DMA((copies,)),
        ],
        compiler_params=pltpu.CompilerParams(
            collective_id=0, has_side_effects=True, vmem_limit_bytes=60 * 1024 * 1024
        ),
    )(
        partner_bits,
        queries.reshape(ROWS, DIM),
        key_tokens.reshape(BLOCK, DIM),
        value_tokens.reshape(BLOCK, DIM),
        output_gradient.reshape(ROWS, DIM),
        summary_proj,
    )
    return (
        out.reshape(queries.shape),
        dq.reshape(queries.shape),
        dk.reshape(key_tokens.shape),
        dv.reshape(value_tokens.shape),
        dproj,
    )


def solution(mesh):
    rows = P("head", "seq", None)
    return jax.shard_map(
        per_device,
        mesh=mesh,
        in_specs=(rows, rows, rows, rows, P(None, "seq"), P("seq", None)),
        out_specs=(rows, rows, rows, rows, P("head", "seq")),
        check_vma=False,
    )
```

```python
import functools
import math

import jax
import jax.numpy as jnp
from jax import lax
from jax.experimental import pallas as pl
from jax.experimental.pallas import tpu as pltpu
from jax.sharding import PartitionSpec as P

MESH = pl.DeviceIdType.MESH
BLOCK = 512
DIM = 128
ROWS = 1024
SUM = 256
CHUNK = 512
SCALE = 1.0 / 12.0
COPIES = 100
EXP2_SCALE = math.log2(math.e) / 12.0
F32, BF16 = jnp.float32, jnp.bfloat16

ORDER = (3, 0, 4, 1, 2)
Z_MASKS = tuple(range(1, 8))
X_MASKS = (8, 16, 24)
HEAD_MASKS = (1, 4, 5, 8, 9, 12, 13)

OWN, SLOT, SUMMARY = 0, 1, 5


def flipped(index, mask):
    out = index
    bit = 1
    while bit <= mask:
        if mask & bit:
            out = out + bit * (1 - 2 * lax.rem(lax.div(index, bit), 2))
        bit *= 2
    return out


def dot(a, b):
    return lax.dot_general(a, b, (((1,), (0,)), ((), ())), preferred_element_type=F32)


def dot_nt(a, b):
    return lax.dot_general(a, b, (((1,), (1,)), ((), ())), preferred_element_type=F32)


def dot_tn(a, b):
    return lax.dot_general(a, b, (((0,), (0,)), ((), ())), preferred_element_type=F32)


def kernel(
    bits_ref, q_ref, k_ref, v_ref, do_ref, proj_ref,
    out_ref, dq_ref, dk_ref, dv_ref, dproj_ref,
    qt, dot_t, part, rx, xsum, zin, half, zbuf, agx,
    kr, vr, ks, vs, e_ref, m_ref, l_ref, mslot, acc, dqt,
    gka, gva, own_gk, own_gv, gslot_k, gslot_v, gk, gv, rgk, rgv,
    part2, rx2, xsum2, zin2, half2, zbuf2, agx2,
    t_ref, rt, w_ref, wb, rh,
    send_sem, recv_sem, edge_sem, hi_sem,
):
    seq = lax.axis_index("seq")
    head = lax.axis_index("head")
    my_x, my_z = lax.div(seq, 8), lax.rem(seq, 8)
    my_y, my_hi, my_core = lax.div(head, 4), lax.rem(lax.div(head, 2), 2), lax.rem(head, 2)
    middle = (my_z == 3) | (my_z == 4)

    barrier = pltpu.get_barrier_semaphore()

    def greet(device):
        pl.semaphore_signal(barrier, inc=1, device_id=device, device_id_type=MESH)

    for mask in (1, 2, 4) + X_MASKS:
        greet({"seq": flipped(seq, mask)})
    for mask in HEAD_MASKS:
        greet({"head": flipped(head, mask)})
    for mask in (3, 5, 6, 7):
        other = flipped(my_z, mask)

        @pl.when(middle | (other == 3) | (other == 4))
        def _():
            greet({"seq": flipped(seq, mask)})

    @pl.when(my_z == 0)
    def _():
        greet({"seq": seq + 7, "head": flipped(head, 2)})

    @pl.when(my_z == 7)
    def _():
        greet({"seq": seq - 7, "head": flipped(head, 2)})

    ids = iter(range(COPIES))
    sent = []

    def start(c):
        c.start()
        sent.append(c)
        return c

    def describe(src, dst, device, n, m):
        return pltpu.make_async_remote_copy(
            src_ref=src, dst_ref=dst, send_sem=send_sem.at[n], recv_sem=recv_sem.at[m],
            device_id=device, device_id_type=MESH,
        )

    def copy(src, dst, axis, mask):
        n = next(ids)
        return start(describe(src, dst, {axis: flipped(seq if axis == "seq" else head, mask)}, n, n))

    def wait_recv(cs):
        for c in cs:
            c.wait_recv()

    proj = proj_ref[...]
    part[0:2] = dot(proj, k_ref[...]).reshape(2, 2, 64, DIM)
    part[2:4] = dot(proj, v_ref[...]).reshape(2, 2, 64, DIM)
    qt[...] = q_ref[...].T
    dot_t[...] = do_ref[...].T

    missing = 10 - (bits_ref[0, 0] + bits_ref[0, 1] + bits_ref[0, 2] + bits_ref[0, 3])
    place = jnp.int32(0)
    for i, b in enumerate(ORDER):
        place = place + jnp.where(missing == b, i, 0)

    at_ends = lax.div(my_z, 7) + lax.div(7 - my_z, 7)
    at_middle = lax.rem(lax.div(my_z + 1, 4), 2) * lax.rem(lax.div(8 - my_z, 4), 2)
    pl.semaphore_wait(barrier, 4 + 3 * at_middle + at_ends + len(X_MASKS) + len(HEAD_MASKS))

    def fetch(i, lo=0, n=BLOCK):
        mask = 1 << ORDER[i]
        return (
            copy(k_ref.at[lo : lo + n], kr.at[i, lo : lo + n], "seq", mask),
            copy(v_ref.at[lo : lo + n], vr.at[i, lo : lo + n], "seq", mask),
        )

    def scatter_x(src, dst):
        return [
            copy(src.at[lax.div(flipped(seq, m), 8)], dst.at[j], "seq", m)
            for j, m in enumerate(X_MASKS)
        ]

    def gather_x(src, dst):
        return [copy(src, dst.at[my_x], "seq", m) for m in X_MASKS]

    def reduce_z(halves, into):
        sends = [next(ids) for _ in range(2)]
        first = [next(ids) for _ in range(7)][0]
        for r in range(2):
            apart = flipped(my_z, 3 + r)

            @pl.when(my_z != 3 + r)
            def _():
                describe(
                    halves.at[r], into.at[apart - 1], {"seq": seq - my_z + (3 + r)}, sends[r], first + apart - 1
                ).start()

        def end():
            for r in range(2):
                @pl.when(my_z != 3 + r)
                def _():
                    describe(halves.at[r], into.at[0], {"seq": flipped(seq, 1)}, sends[r], first).wait_send()

        closing.append(end)
        return first

    def share_z(first, sums, into, buf):
        sends = [next(ids) for _ in range(7)]
        arrive = [next(ids) for _ in range(2)]

        @pl.when(middle)
        def _():
            r = my_z - 3
            total = sums[r]
            for j in range(7):
                describe(buf.at[0], into.at[j], {"seq": flipped(seq, 1)}, sends[0], first + j).wait_recv()
                total = total + into[j].astype(F32)
            buf[r] = total.astype(BF16)
            for j, m in enumerate(Z_MASKS):
                describe(buf.at[r], buf.at[r], {"seq": flipped(seq, m)}, sends[j], arrive[0] + r).start()

        def arrived():
            for r in range(2):
                @pl.when(my_z != 3 + r)
                def _():
                    describe(buf.at[r], buf.at[r], {"seq": flipped(seq, 1)}, sends[0], arrive[r]).wait_recv()

        def end():
            @pl.when(middle)
            def _():
                for j in range(7):
                    describe(buf.at[0], buf.at[0], {"seq": flipped(seq, 1)}, sends[j], arrive[0]).wait_send()

        closing.append(end)
        return arrived

    closing = []

    def forward(row, n, k, v, first=False):
        base = row * BLOCK

        def step(c, carry):
            cols = pl.ds(pl.multiple_of(c * CHUNK, CHUNK), CHUNK)
            s = dot(k[...], qt[:, cols])
            top = jnp.max(s, axis=0, keepdims=True)
            if not first:
                before = m_ref[:, cols]
                top = jnp.maximum(before, top)
                alpha = jnp.exp2((before - top) * EXP2_SCALE)
            e = jnp.exp2((s - top) * EXP2_SCALE)
            total = jnp.sum(e, axis=0, keepdims=True)
            eb = e.astype(BF16)
            e_ref[base : base + n, cols] = eb
            mixed = dot_tn(v[...], eb)
            if not first:
                total = l_ref[:, cols] * alpha + total
                mixed = acc[:, cols] * alpha + mixed
            l_ref[:, cols] = total
            acc[:, cols] = mixed
            m_ref[:, cols] = top
            mslot[row : row + 1, cols] = top
            return carry

        lax.fori_loop(0, ROWS // CHUNK, step, 0)

    def choose(i):
        early = i < place
        ks[i] = jnp.where(early, kr[i], kr[i + 1])
        vs[i] = jnp.where(early, vr[i], vr[i + 1])

    xs = scatter_x(part, rx)
    f_x1 = fetch(0)
    f_x2 = fetch(2)
    f_z4 = fetch(4, 0, 128)
    forward(OWN, BLOCK, k_ref, v_ref, first=True)
    wait_recv(xs)
    xsum[...] = part[my_x] + rx[0] + rx[1] + rx[2]
    half[...] = xsum[...].astype(BF16)
    at_three = reduce_z(half, zin)
    f_z1 = fetch(1)
    gathered = share_z(at_three, xsum, zin, zbuf)
    f_z4 += fetch(4, 128, 128)
    f_z2 = fetch(3)
    f_z4 += fetch(4, 256, 256)
    wait_recv(f_x1 + f_z1)
    choose(0)
    forward(SLOT, BLOCK, ks.at[0], vs.at[0])
    gathered()
    xg = gather_x(zbuf, agx)
    agx[my_x] = zbuf[...]

    @pl.when(my_z == 7)
    def _():
        pl.semaphore_signal(
            edge_sem, inc=1, device_id={"seq": seq - 7, "head": flipped(head, 2)}, device_id_type=MESH
        )

    wait_recv(f_x2)
    choose(1)
    forward(SLOT + 1, BLOCK, ks.at[1], vs.at[1])
    wait_recv(xg)
    sk, sv = ks.at[4, 0:SUM], vs.at[4, 0:SUM]
    sk[...] = agx[0:2].reshape(SUM, DIM)
    sv[...] = agx[2:4].reshape(SUM, DIM)
    forward(SUMMARY, SUM, sk, sv)

    @pl.when(my_z == 0)
    def _():
        pl.semaphore_wait(edge_sem, 1)
        for m in Z_MASKS:
            pl.semaphore_signal(hi_sem, inc=1, device_id={"seq": seq + m}, device_id_type=MESH)

    wait_recv(f_z2)
    choose(2)
    forward(SLOT + 2, BLOCK, ks.at[2], vs.at[2])
    wait_recv(f_z4)
    choose(3)
    forward(SLOT + 3, BLOCK, ks.at[3], vs.at[3])

    inverse = 1.0 / l_ref[...]
    attended = acc[...] * inverse
    delta = jnp.sum(attended * dot_t[...].astype(F32), axis=0, keepdims=True)
    l_ref[...] = inverse
    acc[0:1, :] = delta
    out_ref[...] = attended.T.astype(BF16)
    dqt[...] = jnp.zeros_like(dqt)

    def backward(row, n, k, v, gk_acc, gv_acc):
        base = row * BLOCK
        gk_acc[...] = jnp.zeros_like(gk_acc)
        gv_acc[...] = jnp.zeros_like(gv_acc)

        def step(c, carry):
            cols = pl.ds(pl.multiple_of(c * CHUNK, CHUNK), CHUNK)
            factor = jnp.exp2((mslot[row : row + 1, cols] - m_ref[:, cols]) * EXP2_SCALE) * l_ref[:, cols]
            p = e_ref[base : base + n, cols].astype(F32) * factor
            dp = dot(v[...], dot_t[:, cols])
            ds = (p * (dp - acc[0:1, cols])).astype(BF16)
            dqt[:, cols] += dot_tn(k[...], ds)
            gk_acc[...] += dot(ds, q_ref[cols, :])
            gv_acc[...] += dot(p.astype(BF16), do_ref[cols, :])
            return carry

        lax.fori_loop(0, ROWS // CHUNK, step, 0)

    half_k, half_v = gka.at[0:SUM], gva.at[0:SUM]
    backward(SUMMARY, SUM, sk, sv, half_k, half_v)
    part2[0:2] = (half_k[...] * SCALE).astype(BF16).reshape(2, 2, 64, DIM)
    part2[2:4] = half_v[...].astype(BF16).reshape(2, 2, 64, DIM)
    xs = scatter_x(part2, rx2)

    def slot_back(i):
        backward(SLOT + i, BLOCK, ks.at[i], vs.at[i], gka, gva)
        gslot_k[i] = (gka[...] * SCALE).astype(BF16)
        gslot_v[i] = gva[...].astype(BF16)

    def prepare(i):
        for slots, g in ((gslot_k, gk), (gslot_v, gv)):
            zero = jnp.zeros((BLOCK, DIM), BF16)
            early = slots[i] if i < 4 else zero
            late = slots[i - 1] if i > 0 else zero
            g[i] = jnp.where(i < place, early, jnp.where(i > place, late, zero))

    def give_back(i, lo=0, n=BLOCK):
        mask = 1 << ORDER[i]
        return (
            copy(gk.at[i, lo : lo + n], rgk.at[i, lo : lo + n], "seq", mask),
            copy(gv.at[i, lo : lo + n], rgv.at[i, lo : lo + n], "seq", mask),
        )

    slot_back(3)
    prepare(4)
    wait_recv(xs)
    xsum2[...] = (
        part2[my_x].astype(F32) + rx2[0].astype(F32) + rx2[1].astype(F32) + rx2[2].astype(F32)
    )
    half2[...] = xsum2[...].astype(BF16)
    at_three = reduce_z(half2, zin2)
    r_z4 = give_back(4, 0, 128)
    slot_back(2)
    slot_back(1)
    gathered = share_z(at_three, xsum2, zin2, zbuf2)
    r_z4 += give_back(4, 128, 128)
    prepare(3)
    r_z2 = give_back(3)
    prepare(2)
    r_x2 = give_back(2)
    slot_back(0)
    prepare(0)
    r_x1 = give_back(0)
    prepare(1)
    gathered()
    xg = gather_x(zbuf2, agx2)
    agx2[my_x] = zbuf2[...]
    r_z4 += give_back(4, 256, 128)
    backward(OWN, BLOCK, k_ref, v_ref, own_gk, own_gv)
    wait_recv(xg)
    sg_k = agx2[0:2].reshape(SUM, DIM)
    sg_v = agx2[2:4].reshape(SUM, DIM)
    term = dot_nt(sg_k, k_ref[...]) + dot_nt(sg_v, v_ref[...])
    term = term.astype(BF16).reshape(4, 2, 2, 16, BLOCK)
    t_ref[:, 0] = term[:, :, 0]
    t_ref[:, 1] = term[:, :, 1]

    def term_of(h):
        return t_ref.at[lax.div(h, 4), lax.rem(h, 2)]

    ts = [
        copy(term_of(flipped(head, m)), rt.at[j], "head", m) for j, m in enumerate(HEAD_MASKS)
    ]
    own_gk[...] = own_gk[...] * SCALE + dot_tn(proj_ref[...], sg_k)
    own_gv[...] = own_gv[...] + dot_tn(proj_ref[...], sg_v)
    dq_ref[...] = (dqt[...] * SCALE).T.astype(BF16)
    wait_recv(ts)
    total = t_ref[my_y, my_core].astype(F32)
    for j in range(7):
        total = total + rt[j].astype(F32)
    w_ref[...] = total
    wb[...] = w_ref[1 - my_hi].astype(BF16)

    @pl.when(my_z != 0)
    def _():
        pl.semaphore_wait(hi_sem, 1)

    hs = copy(wb, rh, "head", 2)
    r_z4 += give_back(4, 384, 128)
    r_z1 = give_back(1)
    for c, i in ((r_x1, 0), (r_x2, 2), (r_z2, 3), (r_z1, 1)):
        wait_recv(c)
        own_gk[...] += rgk[i].astype(F32)
        own_gv[...] += rgv[i].astype(F32)
    wait_recv(r_z4)
    dk_ref[...] = (own_gk[...] + rgk[4].astype(F32)).astype(BF16)
    dv_ref[...] = (own_gv[...] + rgv[4].astype(F32)).astype(BF16)
    hs.wait_recv()
    dproj_ref[...] = w_ref[my_hi] + rh[...].astype(F32)
    for c in sent:
        c.wait_send()
    for end in closing:
        end()


def per_device(queries, key_tokens, value_tokens, output_gradient, summary_proj, partner_bits):
    vmem = pl.BlockSpec(memory_space=pltpu.VMEM)
    smem = pl.BlockSpec(memory_space=pltpu.SMEM)
    V = pltpu.VMEM
    out, dq, dk, dv, dproj = pl.pallas_call(
        kernel,
        name="butterfly",
        out_shape=(
            jax.ShapeDtypeStruct((ROWS, DIM), BF16),
            jax.ShapeDtypeStruct((ROWS, DIM), BF16),
            jax.ShapeDtypeStruct((BLOCK, DIM), BF16),
            jax.ShapeDtypeStruct((BLOCK, DIM), BF16),
            jax.ShapeDtypeStruct((16, BLOCK), F32),
        ),
        in_specs=[smem] + [vmem] * 5,
        out_specs=[vmem] * 5,
        scratch_shapes=[
            V((DIM, ROWS), BF16), V((DIM, ROWS), BF16),
            V((4, 2, 64, DIM), F32), V((3, 2, 64, DIM), F32),
            V((2, 64, DIM), F32), V((7, 64, DIM), BF16),
            V((2, 64, DIM), BF16), V((2, 64, DIM), BF16), V((4, 2, 64, DIM), BF16),
            V((5, BLOCK, DIM), BF16), V((5, BLOCK, DIM), BF16),
            V((5, BLOCK, DIM), BF16), V((5, BLOCK, DIM), BF16),
            V((5 * BLOCK + SUM, ROWS), BF16),
            V((1, ROWS), F32), V((1, ROWS), F32), V((8, ROWS), F32),
            V((DIM, ROWS), F32), V((DIM, ROWS), F32),
            V((BLOCK, DIM), F32), V((BLOCK, DIM), F32),
            V((BLOCK, DIM), F32), V((BLOCK, DIM), F32),
            V((4, BLOCK, DIM), BF16), V((4, BLOCK, DIM), BF16),
            V((5, BLOCK, DIM), BF16), V((5, BLOCK, DIM), BF16),
            V((5, BLOCK, DIM), BF16), V((5, BLOCK, DIM), BF16),
            V((4, 2, 64, DIM), BF16), V((3, 2, 64, DIM), BF16),
            V((2, 64, DIM), F32), V((7, 64, DIM), BF16),
            V((2, 64, DIM), BF16), V((2, 64, DIM), BF16), V((4, 2, 64, DIM), BF16),
            V((4, 2, 2, 16, BLOCK), BF16), V((7, 2, 16, BLOCK), BF16),
            V((2, 16, BLOCK), F32), V((16, BLOCK), BF16), V((16, BLOCK), BF16),
            pltpu.SemaphoreType.DMA((COPIES,)), pltpu.SemaphoreType.DMA((COPIES,)),
            pltpu.SemaphoreType.REGULAR, pltpu.SemaphoreType.REGULAR,
        ],
        compiler_params=pltpu.CompilerParams(
            collective_id=0, has_side_effects=True, vmem_limit_bytes=60 * 1024 * 1024
        ),
    )(
        partner_bits,
        queries.reshape(ROWS, DIM),
        key_tokens.reshape(BLOCK, DIM),
        value_tokens.reshape(BLOCK, DIM),
        output_gradient.reshape(ROWS, DIM),
        summary_proj,
    )
    return (
        out.reshape(queries.shape),
        dq.reshape(queries.shape),
        dk.reshape(key_tokens.shape),
        dv.reshape(value_tokens.shape),
        dproj,
    )


def solution(mesh):
    rows = P("head", "seq", None)
    return jax.shard_map(
        per_device,
        mesh=mesh,
        in_specs=(rows, rows, rows, rows, P(None, "seq"), P("seq", None)),
        out_specs=(rows, rows, rows, rows, P("head", "seq")),
        check_vma=False,
    )
```

```python
import functools
import math

import jax
import jax.numpy as jnp
from jax import lax
from jax.experimental import pallas as pl
from jax.experimental.pallas import tpu as pltpu
from jax.sharding import PartitionSpec as P

MESH = pl.DeviceIdType.MESH
BLOCK = 512
DIM = 128
ROWS = 1024
SUM = 256
CHUNK = 512
SCALE = 1.0 / 12.0
COPIES = 120
EXP2_SCALE = math.log2(math.e) / 12.0
F32, BF16 = jnp.float32, jnp.bfloat16

LAST = {0: 4, 1: 5, 2: 6, 3: 7, 4: 6, 5: 7, 6: 7}
RELAY_IN = {s: [z for z in range(s, 8) if LAST[z - s] >= z] for s in (1, 2, 3, 4)}
RELAY_OUT = {s: [z - 1 for z in RELAY_IN[s]] for s in (1, 2, 3, 4)}

ORDER = (3, 0, 4, 1, 2)
Z_MASKS = tuple(range(1, 8))
X_MASKS = (8, 16, 24)
HEAD_MASKS = (1, 4, 5, 8, 9, 12, 13)

OWN, SLOT, SUMMARY = 0, 1, 5


def flipped(index, mask):
    out = index
    bit = 1
    while bit <= mask:
        if mask & bit:
            out = out + bit * (1 - 2 * lax.rem(lax.div(index, bit), 2))
        bit *= 2
    return out


def dot(a, b):
    return lax.dot_general(a, b, (((1,), (0,)), ((), ())), preferred_element_type=F32)


def dot_nt(a, b):
    return lax.dot_general(a, b, (((1,), (1,)), ((), ())), preferred_element_type=F32)


def dot_tn(a, b):
    return lax.dot_general(a, b, (((0,), (0,)), ((), ())), preferred_element_type=F32)


def kernel(
    bits_ref, q_ref, k_ref, v_ref, do_ref, proj_ref,
    out_ref, dq_ref, dk_ref, dv_ref, dproj_ref,
    qt, dot_t, part, rx, xsum, zin, half, zbuf, agx,
    kx, vx, kz, vz, ks, vs, e_ref, m_ref, l_ref, mslot, acc, dqt,
    gka, gva, own_gk, own_gv, gslot_k, gslot_v, gk, gv, rgk, rgv, zsk, zsv, zrk, zrv,
    part2, rx2, xsum2, zin2, half2, zbuf2, agx2,
    t_ref, rt, w_ref, wb, rh,
    send_sem, recv_sem, near_sem, edge_sem, hi_sem,
):
    seq = lax.axis_index("seq")
    head = lax.axis_index("head")
    my_x, my_z = lax.div(seq, 8), lax.rem(seq, 8)
    my_y, my_hi, my_core = lax.div(head, 4), lax.rem(lax.div(head, 2), 2), lax.rem(head, 2)
    middle = (my_z == 3) | (my_z == 4)

    barrier = pltpu.get_barrier_semaphore()

    def greet(device):
        pl.semaphore_signal(barrier, inc=1, device_id=device, device_id_type=MESH)

    for mask in X_MASKS:
        greet({"seq": flipped(seq, mask)})
    for mask in HEAD_MASKS:
        greet({"head": flipped(head, mask)})

    @pl.when(my_z < 7)
    def _():
        greet({"seq": seq + 1})

    @pl.when(my_z > 0)
    def _():
        greet({"seq": seq - 1})

    @pl.when(my_z == 0)
    def _():
        greet({"seq": seq + 7, "head": flipped(head, 2)})

    @pl.when(my_z == 7)
    def _():
        greet({"seq": seq - 7, "head": flipped(head, 2)})

    def one_of(places, mirrored=False):
        found = None
        for z in places:
            here = my_z == (7 - z if mirrored else z)
            found = here if found is None else found | here
        return found

    closing = []
    ids = iter(range(COPIES))
    sent = []

    def start(c):
        c.start()
        sent.append(c)
        return c

    def describe(src, dst, device, n, m):
        return pltpu.make_async_remote_copy(
            src_ref=src, dst_ref=dst, send_sem=send_sem.at[n], recv_sem=recv_sem.at[m],
            device_id=device, device_id_type=MESH,
        )

    def copy(src, dst, axis, mask):
        n = next(ids)
        return start(describe(src, dst, {axis: flipped(seq if axis == "seq" else head, mask)}, n, n))

    def wait_recv(cs):
        for c in cs:
            c.wait_recv()

    proj = proj_ref[...]
    part[0:2] = dot(proj, k_ref[...]).reshape(2, 2, 64, DIM)
    part[2:4] = dot(proj, v_ref[...]).reshape(2, 2, 64, DIM)
    qt[...] = q_ref[...].T
    dot_t[...] = do_ref[...].T

    missing = 10 - (bits_ref[0, 0] + bits_ref[0, 1] + bits_ref[0, 2] + bits_ref[0, 3])
    place = jnp.int32(0)
    for i, b in enumerate(ORDER):
        place = place + jnp.where(missing == b, i, 0)

    pl.semaphore_wait(barrier, 2 + len(X_MASKS) + len(HEAD_MASKS))

    def tell(n):
        for way, there in ((0, my_z < 7), (1, my_z > 0)):
            @pl.when(there)
            def _():
                pl.semaphore_signal(
                    near_sem.at[2 * n + way], inc=1, device_id={"seq": seq + 1 - 2 * way}, device_id_type=MESH
                )

    def hear(n):
        for way, there in ((0, my_z > 0), (1, my_z < 7)):
            @pl.when(there)
            def _():
                pl.semaphore_wait(near_sem.at[2 * n + way], 1)

    def fetch(j, mask):
        return (
            copy(k_ref, kx.at[j], "seq", mask),
            copy(v_ref, vx.at[j], "seq", mask),
        )

    def relay(source, into, n):
        pieces = []
        for way in (0, 1):
            i = next(ids)
            device = {"seq": seq + 1 - 2 * way}
            pieces.append((way, i, device))

        def c(way, i, device):
            return describe(source(way), into(way), device, i, i)

        def go(senders):
            for way, i, device in pieces:
                @pl.when(one_of(senders, way == 1))
                def _():
                    c(way, i, device).start()

            def end():
                for way, i, device in pieces:
                    @pl.when(one_of(senders, way == 1))
                    def _():
                        c(way, i, device).wait_send()

            closing.append(end)

        def arrived(receivers):
            for way, i, device in pieces:
                @pl.when(one_of(receivers, way == 1))
                def _():
                    c(way, i, device).wait_recv()

        return go, arrived

    def fetch_z(own, into):
        steps = []
        for n in (1, 2, 3, 4):
            source = (lambda way: own) if n == 1 else (lambda way, n=n: into.at[way, n - 2])
            steps.append(relay(source, lambda way, n=n: into.at[way, n - 1], n))

        def go(n):
            if n > 1:
                steps[n - 2][1](RELAY_IN[n - 1])
            if n <= 4:
                steps[n - 1][0](RELAY_OUT[n])

        return go

    def scatter_x(src, dst):
        return [
            copy(src.at[lax.div(flipped(seq, m), 8)], dst.at[j], "seq", m)
            for j, m in enumerate(X_MASKS)
        ]

    def gather_x(src, dst):
        return [copy(src, dst.at[my_x], "seq", m) for m in X_MASKS]

    def reduce_z(halves, into):
        sends = [next(ids) for _ in range(2)]
        first = [next(ids) for _ in range(7)][0]
        for r in range(2):
            apart = flipped(my_z, 3 + r)

            @pl.when(my_z != 3 + r)
            def _():
                describe(
                    halves.at[r], into.at[apart - 1], {"seq": seq - my_z + (3 + r)}, sends[r], first + apart - 1
                ).start()

        def end():
            for r in range(2):
                @pl.when(my_z != 3 + r)
                def _():
                    describe(halves.at[r], into.at[0], {"seq": flipped(seq, 1)}, sends[r], first).wait_send()

        closing.append(end)
        return first

    def share_z(first, sums, into, buf):
        sends = [next(ids) for _ in range(7)]
        arrive = [next(ids) for _ in range(2)]

        @pl.when(middle)
        def _():
            r = my_z - 3
            total = sums[r]
            for j in range(7):
                describe(buf.at[0], into.at[j], {"seq": flipped(seq, 1)}, sends[0], first + j).wait_recv()
                total = total + into[j].astype(F32)
            buf[r] = total.astype(BF16)
            for j, m in enumerate(Z_MASKS):
                describe(buf.at[r], buf.at[r], {"seq": flipped(seq, m)}, sends[j], arrive[0] + r).start()

        def arrived():
            for r in range(2):
                @pl.when(my_z != 3 + r)
                def _():
                    describe(buf.at[r], buf.at[r], {"seq": flipped(seq, 1)}, sends[0], arrive[r]).wait_recv()

        def end():
            @pl.when(middle)
            def _():
                for j in range(7):
                    describe(buf.at[0], buf.at[0], {"seq": flipped(seq, 1)}, sends[j], arrive[0]).wait_send()

        closing.append(end)
        return arrived

    def forward(row, n, k, v, first=False):
        base = row * BLOCK

        def step(c, carry):
            cols = pl.ds(pl.multiple_of(c * CHUNK, CHUNK), CHUNK)
            s = dot(k[...], qt[:, cols])
            top = jnp.max(s, axis=0, keepdims=True)
            if not first:
                before = m_ref[:, cols]
                top = jnp.maximum(before, top)
                alpha = jnp.exp2((before - top) * EXP2_SCALE)
            e = jnp.exp2((s - top) * EXP2_SCALE)
            total = jnp.sum(e, axis=0, keepdims=True)
            eb = e.astype(BF16)
            e_ref[base : base + n, cols] = eb
            mixed = dot_tn(v[...], eb)
            if not first:
                total = l_ref[:, cols] * alpha + total
                mixed = acc[:, cols] * alpha + mixed
            l_ref[:, cols] = total
            acc[:, cols] = mixed
            m_ref[:, cols] = top
            mslot[row : row + 1, cols] = top
            return carry

        lax.fori_loop(0, ROWS // CHUNK, step, 0)

    from_above = [1 - lax.rem(lax.div(my_z, b), 2) for b in (1, 2, 4)]

    def partner(i, x, z):
        if ORDER[i] >= 3:
            return x[ORDER[i] - 3]
        bit = ORDER[i]
        return z[from_above[bit], (1 << bit) - 1]

    def choose(i):
        early = i < place
        ks[i] = jnp.where(early, partner(i, kx, kz), partner(i + 1, kx, kz))
        vs[i] = jnp.where(early, partner(i, vx, vz), partner(i + 1, vx, vz))

    go_k, go_v = fetch_z(k_ref, kz), fetch_z(v_ref, vz)
    go_k(1)
    go_v(1)
    tell(0)
    xs = scatter_x(part, rx)
    f_x1 = fetch(0, 8)
    f_x2 = fetch(1, 16)
    forward(OWN, BLOCK, k_ref, v_ref, first=True)
    hear(0)
    tell(1)
    go_k(2)
    hear(1)
    tell(2)
    wait_recv(xs)
    xsum[...] = part[my_x] + rx[0] + rx[1] + rx[2]
    half[...] = xsum[...].astype(BF16)
    hear(2)
    at_three = reduce_z(half, zin)
    go_v(2)
    wait_recv(f_x1)
    choose(0)
    forward(SLOT, BLOCK, ks.at[0], vs.at[0])
    go_k(3)
    gathered = share_z(at_three, xsum, zin, zbuf)
    go_v(3)
    wait_recv(f_x2)
    choose(1)
    forward(SLOT + 1, BLOCK, ks.at[1], vs.at[1])
    go_k(4)
    gathered()
    xg = gather_x(zbuf, agx)
    agx[my_x] = zbuf[...]
    go_v(4)
    choose(2)
    forward(SLOT + 2, BLOCK, ks.at[2], vs.at[2])

    @pl.when(my_z == 7)
    def _():
        pl.semaphore_signal(
            edge_sem, inc=1, device_id={"seq": seq - 7, "head": flipped(head, 2)}, device_id_type=MESH
        )

    wait_recv(xg)
    sk, sv = ks.at[4, 0:SUM], vs.at[4, 0:SUM]
    sk[...] = agx[0:2].reshape(SUM, DIM)
    sv[...] = agx[2:4].reshape(SUM, DIM)
    forward(SUMMARY, SUM, sk, sv)

    @pl.when(my_z == 0)
    def _():
        pl.semaphore_wait(edge_sem, 1)
        for m in Z_MASKS:
            pl.semaphore_signal(hi_sem, inc=1, device_id={"seq": seq + m}, device_id_type=MESH)

    go_k(5)
    go_v(5)
    choose(3)
    forward(SLOT + 3, BLOCK, ks.at[3], vs.at[3])

    inverse = 1.0 / l_ref[...]
    attended = acc[...] * inverse
    delta = jnp.sum(attended * dot_t[...].astype(F32), axis=0, keepdims=True)
    l_ref[...] = inverse
    acc[0:1, :] = delta
    out_ref[...] = attended.T.astype(BF16)
    dqt[...] = jnp.zeros_like(dqt)

    def backward(row, n, k, v, gk_acc, gv_acc):
        base = row * BLOCK
        gk_acc[...] = jnp.zeros_like(gk_acc)
        gv_acc[...] = jnp.zeros_like(gv_acc)

        def step(c, carry):
            cols = pl.ds(pl.multiple_of(c * CHUNK, CHUNK), CHUNK)
            factor = jnp.exp2((mslot[row : row + 1, cols] - m_ref[:, cols]) * EXP2_SCALE) * l_ref[:, cols]
            p = e_ref[base : base + n, cols].astype(F32) * factor
            dp = dot(v[...], dot_t[:, cols])
            ds = (p * (dp - acc[0:1, cols])).astype(BF16)
            dqt[:, cols] += dot_tn(k[...], ds)
            gk_acc[...] += dot(ds, q_ref[cols, :])
            gv_acc[...] += dot(p.astype(BF16), do_ref[cols, :])
            return carry

        lax.fori_loop(0, ROWS // CHUNK, step, 0)

    half_k, half_v = gka.at[0:SUM], gva.at[0:SUM]
    backward(SUMMARY, SUM, sk, sv, half_k, half_v)
    part2[0:2] = (half_k[...] * SCALE).astype(BF16).reshape(2, 2, 64, DIM)
    part2[2:4] = half_v[...].astype(BF16).reshape(2, 2, 64, DIM)
    xs = scatter_x(part2, rx2)

    def slot_back(i):
        backward(SLOT + i, BLOCK, ks.at[i], vs.at[i], gka, gva)
        gslot_k[i] = (gka[...] * SCALE).astype(BF16)
        gslot_v[i] = gva[...].astype(BF16)

    def prepare(i):
        for slots, g in ((gslot_k, gk), (gslot_v, gv)):
            zero = jnp.zeros((BLOCK, DIM), BF16)
            early = slots[i] if i < 4 else zero
            late = slots[i - 1] if i > 0 else zero
            g[i] = jnp.where(i < place, early, jnp.where(i > place, late, zero))

    def give_back(j, i, mask):
        return (
            copy(gk.at[i], rgk.at[j], "seq", mask),
            copy(gv.at[i], rgv.at[j], "seq", mask),
        )

    def return_z(g, sums, into):
        steps = {}
        for n in (4, 3, 2, 1):
            if n == 4:
                source = lambda way: g.at[4]
            elif n == 3:
                source = lambda way: into.at[way, 3]
            else:
                source = lambda way, n=n: sums.at[way, n - 1]
            steps[n] = relay(source, lambda way, n=n: into.at[way, n - 1], n)

        def up_down(places):
            return [7 - z for z in places]

        def go(n):
            if n < 4:
                steps[n + 1][1](up_down(RELAY_OUT[n + 1]))
            if n in (1, 2):
                own_value = g[3 if n == 2 else 1].astype(F32)
                for way in (0, 1):
                    came = one_of(up_down(RELAY_OUT[n + 1]), way == 1)
                    mine = from_above[n - 1] == 1 - way
                    sums[way, n - 1] = (
                        jnp.where(came, into[way, n].astype(F32), 0.0) + jnp.where(mine, own_value, 0.0)
                    ).astype(BF16)
            if n > 0:
                steps[n][0](up_down(RELAY_IN[n]))

        return go

    back_k, back_v = return_z(gk, zsk, zrk), return_z(gv, zsv, zrv)
    slot_back(3)
    prepare(4)
    back_k(4)
    slot_back(2)
    prepare(3)
    wait_recv(xs)
    xsum2[...] = (
        part2[my_x].astype(F32) + rx2[0].astype(F32) + rx2[1].astype(F32) + rx2[2].astype(F32)
    )
    half2[...] = xsum2[...].astype(BF16)
    at_three = reduce_z(half2, zin2)
    back_v(4)
    slot_back(1)
    prepare(2)
    r_x2 = give_back(1, 2, 16)
    back_k(3)
    slot_back(0)
    prepare(0)
    r_x1 = give_back(0, 0, 8)
    prepare(1)
    gathered = share_z(at_three, xsum2, zin2, zbuf2)
    back_v(3)
    back_k(2)
    backward(OWN, BLOCK, k_ref, v_ref, own_gk, own_gv)
    back_v(2)
    gathered()
    xg = gather_x(zbuf2, agx2)
    agx2[my_x] = zbuf2[...]
    dq_ref[...] = (dqt[...] * SCALE).T.astype(BF16)
    back_k(1)
    wait_recv(xg)
    sg_k = agx2[0:2].reshape(SUM, DIM)
    sg_v = agx2[2:4].reshape(SUM, DIM)
    term = dot_nt(sg_k, k_ref[...]) + dot_nt(sg_v, v_ref[...])
    term = term.astype(BF16).reshape(4, 2, 2, 16, BLOCK)
    t_ref[:, 0] = term[:, :, 0]
    t_ref[:, 1] = term[:, :, 1]

    def term_of(h):
        return t_ref.at[lax.div(h, 4), lax.rem(h, 2)]

    ts = [
        copy(term_of(flipped(head, m)), rt.at[j], "head", m) for j, m in enumerate(HEAD_MASKS)
    ]
    own_gk[...] = own_gk[...] * SCALE + dot_tn(proj_ref[...], sg_k)
    own_gv[...] = own_gv[...] + dot_tn(proj_ref[...], sg_v)
    back_v(1)
    wait_recv(ts)
    total = t_ref[my_y, my_core].astype(F32)
    for j in range(7):
        total = total + rt[j].astype(F32)
    w_ref[...] = total
    wb[...] = w_ref[1 - my_hi].astype(BF16)

    @pl.when(my_z != 0)
    def _():
        pl.semaphore_wait(hi_sem, 1)

    hs = copy(wb, rh, "head", 2)
    for c, j in ((r_x1, 0), (r_x2, 1)):
        wait_recv(c)
        own_gk[...] += rgk[j].astype(F32)
        own_gv[...] += rgv[j].astype(F32)
    up_arrives, down_arrives = my_z > 0, my_z < 7
    for back, own, into, result in ((back_k, own_gk, zrk, dk_ref), (back_v, own_gv, zrv, dv_ref)):
        back(0)
        result[...] = (
            own[...]
            + jnp.where(up_arrives, into[0, 0].astype(F32), 0.0)
            + jnp.where(down_arrives, into[1, 0].astype(F32), 0.0)
        ).astype(BF16)
    hs.wait_recv()
    dproj_ref[...] = w_ref[my_hi] + rh[...].astype(F32)
    for c in sent:
        c.wait_send()
    for end in closing:
        end()


def per_device(queries, key_tokens, value_tokens, output_gradient, summary_proj, partner_bits):
    vmem = pl.BlockSpec(memory_space=pltpu.VMEM)
    smem = pl.BlockSpec(memory_space=pltpu.SMEM)
    V = pltpu.VMEM
    out, dq, dk, dv, dproj = pl.pallas_call(
        kernel,
        name="butterfly",
        out_shape=(
            pltpu.VMEM((ROWS, DIM), BF16),
            pltpu.VMEM((ROWS, DIM), BF16),
            pltpu.VMEM((BLOCK, DIM), BF16),
            pltpu.VMEM((BLOCK, DIM), BF16),
            pltpu.VMEM((16, BLOCK), F32),
        ),
        in_specs=[smem] + [vmem] * 5,
        out_specs=[vmem] * 5,
        scratch_shapes=[
            V((DIM, ROWS), BF16), V((DIM, ROWS), BF16),
            V((4, 2, 64, DIM), F32), V((3, 2, 64, DIM), F32),
            V((2, 64, DIM), F32), V((7, 64, DIM), BF16),
            V((2, 64, DIM), BF16), V((2, 64, DIM), BF16), V((4, 2, 64, DIM), BF16),
            V((2, BLOCK, DIM), BF16), V((2, BLOCK, DIM), BF16),
            V((2, 4, BLOCK, DIM), BF16), V((2, 4, BLOCK, DIM), BF16),
            V((5, BLOCK, DIM), BF16), V((5, BLOCK, DIM), BF16),
            V((5 * BLOCK + SUM, ROWS), BF16),
            V((1, ROWS), F32), V((1, ROWS), F32), V((8, ROWS), F32),
            V((DIM, ROWS), F32), V((DIM, ROWS), F32),
            V((BLOCK, DIM), F32), V((BLOCK, DIM), F32),
            V((BLOCK, DIM), F32), V((BLOCK, DIM), F32),
            V((4, BLOCK, DIM), BF16), V((4, BLOCK, DIM), BF16),
            V((5, BLOCK, DIM), BF16), V((5, BLOCK, DIM), BF16),
            V((2, BLOCK, DIM), BF16), V((2, BLOCK, DIM), BF16),
            V((2, 2, BLOCK, DIM), BF16), V((2, 2, BLOCK, DIM), BF16),
            V((2, 4, BLOCK, DIM), BF16), V((2, 4, BLOCK, DIM), BF16),
            V((4, 2, 64, DIM), BF16), V((3, 2, 64, DIM), BF16),
            V((2, 64, DIM), F32), V((7, 64, DIM), BF16),
            V((2, 64, DIM), BF16), V((2, 64, DIM), BF16), V((4, 2, 64, DIM), BF16),
            V((4, 2, 2, 16, BLOCK), BF16), V((7, 2, 16, BLOCK), BF16),
            V((2, 16, BLOCK), F32), V((16, BLOCK), BF16), V((16, BLOCK), BF16),
            pltpu.SemaphoreType.DMA((COPIES,)), pltpu.SemaphoreType.DMA((COPIES,)),
            pltpu.SemaphoreType.REGULAR((6,)), pltpu.SemaphoreType.REGULAR, pltpu.SemaphoreType.REGULAR,
        ],
        compiler_params=pltpu.CompilerParams(
            collective_id=0, has_side_effects=True, vmem_limit_bytes=60 * 1024 * 1024
        ),
    )(
        partner_bits,
        queries.reshape(ROWS, DIM),
        key_tokens.reshape(BLOCK, DIM),
        value_tokens.reshape(BLOCK, DIM),
        output_gradient.reshape(ROWS, DIM),
        summary_proj,
    )
    return (
        out.reshape(queries.shape),
        dq.reshape(queries.shape),
        dk.reshape(key_tokens.shape),
        dv.reshape(value_tokens.shape),
        dproj,
    )


def solution(mesh):
    rows = P("head", "seq", None)
    return jax.shard_map(
        per_device,
        mesh=mesh,
        in_specs=(rows, rows, rows, rows, P(None, "seq"), P("seq", None)),
        out_specs=(rows, rows, rows, rows, P("head", "seq")),
        check_vma=False,
    )
```

```python
import functools
import math

import jax
import jax.numpy as jnp
from jax import lax
from jax.experimental import pallas as pl
from jax.experimental.pallas import tpu as pltpu
from jax.sharding import PartitionSpec as P

MESH = pl.DeviceIdType.MESH
BLOCK = 512
DIM = 128
ROWS = 1024
SUM = 256
CHUNK = 512
SCALE = 1.0 / 12.0
COPIES = 120
EXP2_SCALE = math.log2(math.e) / 12.0
F32, BF16 = jnp.float32, jnp.bfloat16

LAST = {0: 4, 1: 5, 2: 6, 3: 7, 4: 6, 5: 7, 6: 7}
RELAY_IN = {s: [z for z in range(s, 8) if LAST[z - s] >= z] for s in (1, 2, 3, 4)}
RELAY_OUT = {s: [z - 1 for z in RELAY_IN[s]] for s in (1, 2, 3, 4)}

ORDER = (3, 0, 4, 1, 2)
Z_MASKS = tuple(range(1, 8))
X_MASKS = (8, 16, 24)
HEAD_MASKS = (1, 4, 5, 8, 9, 12, 13)

OWN, SLOT, SUMMARY = 0, 1, 5


def flipped(index, mask):
    out = index
    bit = 1
    while bit <= mask:
        if mask & bit:
            out = out + bit * (1 - 2 * lax.rem(lax.div(index, bit), 2))
        bit *= 2
    return out


def dot(a, b):
    return lax.dot_general(a, b, (((1,), (0,)), ((), ())), preferred_element_type=F32)


def dot_nt(a, b):
    return lax.dot_general(a, b, (((1,), (1,)), ((), ())), preferred_element_type=F32)


def dot_tn(a, b):
    return lax.dot_general(a, b, (((0,), (0,)), ((), ())), preferred_element_type=F32)


def kernel(
    bits_ref, q_in, k_in, v_in, do_in, proj_in,
    out_ref, dq_ref, dk_ref, dv_ref, dproj_ref,
    q_ref, k_ref, v_ref, do_ref, proj_ref, load_sem,
    qt, dot_t, part, rx, xsum, zin, half, zbuf, agx,
    kx, vx, kz, vz, ks, vs, e_ref, m_ref, l_ref, mslot, rescale, delta_ref, acc, dqt,
    gka, gva, own_gk, own_gv, gslot_k, gslot_v, gk, gv, rgk, rgv, zsk, zsv, zrk, zrv,
    part2, rx2, xsum2, zin2, half2, zbuf2, agx2,
    t_ref, rt, rt2, w_ref, wb, rh,
    send_sem, recv_sem, near_sem, edge_sem, hi_sem,
):
    seq = lax.axis_index("seq")
    head = lax.axis_index("head")
    my_x, my_z = lax.div(seq, 8), lax.rem(seq, 8)
    my_y, my_hi, my_core = lax.div(head, 4), lax.rem(lax.div(head, 2), 2), lax.rem(head, 2)
    middle = (my_z == 3) | (my_z == 4)

    barrier = pltpu.get_barrier_semaphore()

    def greet(device):
        pl.semaphore_signal(barrier, inc=1, device_id=device, device_id_type=MESH)

    for mask in X_MASKS:
        greet({"seq": flipped(seq, mask)})
    for mask in HEAD_MASKS:
        greet({"head": flipped(head, mask)})

    @pl.when(my_z < 7)
    def _():
        greet({"seq": seq + 1})

    @pl.when(my_z > 0)
    def _():
        greet({"seq": seq - 1})

    @pl.when(my_z == 0)
    def _():
        greet({"seq": seq + 7, "head": flipped(head, 2)})

    @pl.when(my_z == 7)
    def _():
        greet({"seq": seq - 7, "head": flipped(head, 2)})

    loads = [
        pltpu.make_async_copy(src, dst, load_sem.at[n])
        for n, (src, dst) in enumerate(
            ((k_in, k_ref), (v_in, v_ref), (proj_in, proj_ref), (q_in, q_ref), (do_in, do_ref))
        )
    ]
    for load in loads:
        load.start()

    def one_of(places, mirrored=False):
        found = None
        for z in places:
            here = my_z == (7 - z if mirrored else z)
            found = here if found is None else found | here
        return found

    closing = []
    ids = iter(range(COPIES))
    sent = []

    def start(c):
        c.start()
        sent.append(c)
        return c

    def describe(src, dst, device, n, m):
        return pltpu.make_async_remote_copy(
            src_ref=src, dst_ref=dst, send_sem=send_sem.at[n], recv_sem=recv_sem.at[m],
            device_id=device, device_id_type=MESH,
        )

    def copy(src, dst, axis, mask):
        n = next(ids)
        return start(describe(src, dst, {axis: flipped(seq if axis == "seq" else head, mask)}, n, n))

    def wait_recv(cs):
        for c in cs:
            c.wait_recv()

    for load in loads[:3]:
        load.wait()

    proj = proj_ref[...]
    part[0:2] = dot(proj, k_ref[...]).reshape(2, 2, 64, DIM)
    part[2:4] = dot(proj, v_ref[...]).reshape(2, 2, 64, DIM)
    for load in loads[3:]:
        load.wait()
    qt[...] = q_ref[...].T
    dot_t[...] = do_ref[...].T

    missing = 10 - (bits_ref[0, 0] + bits_ref[0, 1] + bits_ref[0, 2] + bits_ref[0, 3])
    place = jnp.int32(0)
    for i, b in enumerate(ORDER):
        place = place + jnp.where(missing == b, i, 0)

    pl.semaphore_wait(barrier, 2 + len(X_MASKS) + len(HEAD_MASKS))

    def tell(n):
        for way, there in ((0, my_z < 7), (1, my_z > 0)):
            @pl.when(there)
            def _():
                pl.semaphore_signal(
                    near_sem.at[2 * n + way], inc=1, device_id={"seq": seq + 1 - 2 * way}, device_id_type=MESH
                )

    def hear(n):
        for way, there in ((0, my_z > 0), (1, my_z < 7)):
            @pl.when(there)
            def _():
                pl.semaphore_wait(near_sem.at[2 * n + way], 1)

    def fetch(j, mask):
        return (
            copy(k_ref, kx.at[j], "seq", mask),
            copy(v_ref, vx.at[j], "seq", mask),
        )

    def relay(source, into, n):
        pieces = []
        for way in (0, 1):
            i = next(ids)
            device = {"seq": seq + 1 - 2 * way}
            pieces.append((way, i, device))

        def c(way, i, device):
            return describe(source(way), into(way), device, i, i)

        def go(senders):
            for way, i, device in pieces:
                @pl.when(one_of(senders, way == 1))
                def _():
                    c(way, i, device).start()

            def end():
                for way, i, device in pieces:
                    @pl.when(one_of(senders, way == 1))
                    def _():
                        c(way, i, device).wait_send()

            closing.append(end)

        def arrived(receivers):
            for way, i, device in pieces:
                @pl.when(one_of(receivers, way == 1))
                def _():
                    c(way, i, device).wait_recv()

        return go, arrived

    def fetch_z(own, into):
        steps = []
        for n in (1, 2, 3, 4):
            source = (lambda way: own) if n == 1 else (lambda way, n=n: into.at[way, n - 2])
            steps.append(relay(source, lambda way, n=n: into.at[way, n - 1], n))

        def go(n):
            if n > 1:
                steps[n - 2][1](RELAY_IN[n - 1])
            if n <= 4:
                steps[n - 1][0](RELAY_OUT[n])

        return go

    def scatter_x(src, dst):
        return [
            copy(src.at[lax.div(flipped(seq, m), 8)], dst.at[j], "seq", m)
            for j, m in enumerate(X_MASKS)
        ]

    def gather_x(src, dst):
        return [copy(src, dst.at[my_x], "seq", m) for m in X_MASKS]

    def reduce_z(halves, into):
        sends = [next(ids) for _ in range(2)]
        first = [next(ids) for _ in range(7)][0]
        for r in range(2):
            apart = flipped(my_z, 3 + r)

            @pl.when(my_z != 3 + r)
            def _():
                describe(
                    halves.at[r], into.at[apart - 1], {"seq": seq - my_z + (3 + r)}, sends[r], first + apart - 1
                ).start()

        def end():
            for r in range(2):
                @pl.when(my_z != 3 + r)
                def _():
                    describe(halves.at[r], into.at[0], {"seq": flipped(seq, 1)}, sends[r], first).wait_send()

        closing.append(end)
        return first

    def share_z(first, sums, into, buf):
        sends = [next(ids) for _ in range(7)]
        arrive = [next(ids) for _ in range(2)]

        @pl.when(middle)
        def _():
            r = my_z - 3
            total = sums[r]
            for j in range(7):
                describe(buf.at[0], into.at[j], {"seq": flipped(seq, 1)}, sends[0], first + j).wait_recv()
                total = total + into[j].astype(F32)
            buf[r] = total.astype(BF16)
            for j, m in enumerate(Z_MASKS):
                describe(buf.at[r], buf.at[r], {"seq": flipped(seq, m)}, sends[j], arrive[0] + r).start()

        def arrived():
            for r in range(2):
                @pl.when(my_z != 3 + r)
                def _():
                    describe(buf.at[r], buf.at[r], {"seq": flipped(seq, 1)}, sends[0], arrive[r]).wait_recv()

        def end():
            @pl.when(middle)
            def _():
                for j in range(7):
                    describe(buf.at[0], buf.at[0], {"seq": flipped(seq, 1)}, sends[j], arrive[0]).wait_send()

        closing.append(end)
        return arrived

    def scores(row, n, k, first=False):
        base = row * BLOCK

        def step(c, carry):
            cols = pl.ds(pl.multiple_of(c * CHUNK, CHUNK), CHUNK)
            s = dot(k[...], qt[:, cols])
            top = jnp.max(s, axis=0, keepdims=True)
            if not first:
                before = m_ref[:, cols]
                top = jnp.maximum(before, top)
                alpha = jnp.exp2((before - top) * EXP2_SCALE)
                rescale[:, cols] = alpha
            e = jnp.exp2((s - top) * EXP2_SCALE)
            total = jnp.sum(e, axis=0, keepdims=True)
            e_ref[base : base + n, cols] = e.astype(BF16)
            if not first:
                total = l_ref[:, cols] * alpha + total
            l_ref[:, cols] = total
            m_ref[:, cols] = top
            mslot[row : row + 1, cols] = top
            return carry

        lax.fori_loop(0, ROWS // CHUNK, step, 0)

    def mix(row, n, v, first=False):
        base = row * BLOCK

        def step(c, carry):
            cols = pl.ds(pl.multiple_of(c * CHUNK, CHUNK), CHUNK)
            mixed = dot_tn(v[...], e_ref[base : base + n, cols])
            if not first:
                mixed = acc[:, cols] * rescale[:, cols] + mixed
            acc[:, cols] = mixed
            return carry

        lax.fori_loop(0, ROWS // CHUNK, step, 0)

    def forward(row, n, k, v, first=False):
        scores(row, n, k, first)
        mix(row, n, v, first)

    from_above = [1 - lax.rem(lax.div(my_z, b), 2) for b in (1, 2, 4)]

    def partner(i, x, z):
        if ORDER[i] >= 3:
            return x[ORDER[i] - 3]
        bit = ORDER[i]
        return z[from_above[bit], (1 << bit) - 1]

    def choose(i, chosen, x, z):
        chosen[i] = jnp.where(i < place, partner(i, x, z), partner(i + 1, x, z))

    go_k, go_v = fetch_z(k_ref, kz), fetch_z(v_ref, vz)
    go_k(1)
    go_v(1)
    tell(0)
    xs = scatter_x(part, rx)
    f_x1 = fetch(0, 8)
    f_x2 = fetch(1, 16)
    forward(OWN, BLOCK, k_ref, v_ref, first=True)
    hear(0)
    tell(1)
    go_k(2)
    hear(1)
    tell(2)
    wait_recv(xs)
    xsum[...] = part[my_x] + rx[0] + rx[1] + rx[2]
    half[...] = xsum[...].astype(BF16)
    hear(2)
    at_three = reduce_z(half, zin)
    go_v(2)
    wait_recv(f_x1)
    choose(0, ks, kx, kz)
    choose(0, vs, vx, vz)
    forward(SLOT, BLOCK, ks.at[0], vs.at[0])
    go_k(3)
    gathered = share_z(at_three, xsum, zin, zbuf)
    go_v(3)
    wait_recv(f_x2)
    choose(1, ks, kx, kz)
    choose(1, vs, vx, vz)
    forward(SLOT + 1, BLOCK, ks.at[1], vs.at[1])
    go_k(4)
    gathered()
    xg = gather_x(zbuf, agx)
    agx[my_x] = zbuf[...]
    go_v(4)
    choose(2, ks, kx, kz)
    choose(2, vs, vx, vz)
    forward(SLOT + 2, BLOCK, ks.at[2], vs.at[2])

    @pl.when(my_z == 7)
    def _():
        pl.semaphore_signal(
            edge_sem, inc=1, device_id={"seq": seq - 7, "head": flipped(head, 2)}, device_id_type=MESH
        )

    dqt[...] = jnp.zeros_like(dqt)
    wait_recv(xg)
    sk, sv = ks.at[4, 0:SUM], vs.at[4, 0:SUM]
    sk[...] = agx[0:2].reshape(SUM, DIM)
    sv[...] = agx[2:4].reshape(SUM, DIM)
    forward(SUMMARY, SUM, sk, sv)

    @pl.when(my_z == 0)
    def _():
        pl.semaphore_wait(edge_sem, 1)
        for m in Z_MASKS:
            pl.semaphore_signal(hi_sem, inc=1, device_id={"seq": seq + m}, device_id_type=MESH)

    go_k(5)
    choose(3, ks, kx, kz)
    scores(SLOT + 3, BLOCK, ks.at[3])
    l_ref[...] = 1.0 / l_ref[...]
    go_v(5)
    choose(3, vs, vx, vz)
    mix(SLOT + 3, BLOCK, vs.at[3])

    attended = acc[...] * l_ref[...]
    delta_ref[...] = jnp.sum(attended * dot_t[...].astype(F32), axis=0, keepdims=True)

    def backward(row, n, k, v, gk_acc, gv_acc):
        base = row * BLOCK
        gk_acc[...] = jnp.zeros_like(gk_acc)
        gv_acc[...] = jnp.zeros_like(gv_acc)

        def step(c, carry):
            cols = pl.ds(pl.multiple_of(c * CHUNK, CHUNK), CHUNK)
            factor = jnp.exp2((mslot[row : row + 1, cols] - m_ref[:, cols]) * EXP2_SCALE) * l_ref[:, cols]
            p = e_ref[base : base + n, cols].astype(F32) * factor
            dp = dot(v[...], dot_t[:, cols])
            ds = (p * (dp - delta_ref[:, cols])).astype(BF16)
            dqt[:, cols] += dot_tn(k[...], ds)
            gk_acc[...] += dot(ds, q_ref[cols, :])
            gv_acc[...] += dot(p.astype(BF16), do_ref[cols, :])
            return carry

        lax.fori_loop(0, ROWS // CHUNK, step, 0)

    half_k, half_v = gka.at[0:SUM], gva.at[0:SUM]
    backward(SUMMARY, SUM, sk, sv, half_k, half_v)
    part2[0:2] = (half_k[...] * SCALE).astype(BF16).reshape(2, 2, 64, DIM)
    part2[2:4] = half_v[...].astype(BF16).reshape(2, 2, 64, DIM)
    xs = scatter_x(part2, rx2)

    def slot_back(i):
        backward(SLOT + i, BLOCK, ks.at[i], vs.at[i], gka, gva)
        gslot_k[i] = (gka[...] * SCALE).astype(BF16)
        gslot_v[i] = gva[...].astype(BF16)

    def prepare(i):
        for slots, g in ((gslot_k, gk), (gslot_v, gv)):
            zero = jnp.zeros((BLOCK, DIM), BF16)
            early = slots[i] if i < 4 else zero
            late = slots[i - 1] if i > 0 else zero
            g[i] = jnp.where(i < place, early, jnp.where(i > place, late, zero))

    def give_back(g, into, j, i, mask):
        return copy(g.at[i], into.at[j], "seq", mask)

    def return_z(g, sums, into):
        steps = {}
        for n in (4, 3, 2, 1):
            if n == 4:
                source = lambda way: g.at[4]
            elif n == 3:
                source = lambda way: into.at[way, 3]
            else:
                source = lambda way, n=n: sums.at[way, n - 1]
            steps[n] = relay(source, lambda way, n=n: into.at[way, n - 1], n)

        def up_down(places):
            return [7 - z for z in places]

        def go(n):
            if n < 4:
                steps[n + 1][1](up_down(RELAY_OUT[n + 1]))
            if n in (1, 2):
                own_value = g[3 if n == 2 else 1].astype(F32)
                for way in (0, 1):
                    came = one_of(up_down(RELAY_OUT[n + 1]), way == 1)
                    mine = from_above[n - 1] == 1 - way
                    sums[way, n - 1] = (
                        jnp.where(came, into[way, n].astype(F32), 0.0) + jnp.where(mine, own_value, 0.0)
                    ).astype(BF16)
            if n > 0:
                steps[n][0](up_down(RELAY_IN[n]))

        return go

    back_k, back_v = return_z(gk, zsk, zrk), return_z(gv, zsv, zrv)
    out_ref[...] = (acc[...] * l_ref[...]).T.astype(BF16)
    slot_back(3)
    prepare(4)
    wait_recv(xs)
    xsum2[...] = (
        part2[my_x].astype(F32) + rx2[0].astype(F32) + rx2[1].astype(F32) + rx2[2].astype(F32)
    )
    half2[...] = xsum2[...].astype(BF16)
    at_three = reduce_z(half2, zin2)
    back_k(4)
    back_v(4)
    slot_back(2)
    prepare(3)
    slot_back(1)
    prepare(2)
    r_x2 = [give_back(gk, rgk, 1, 2, 16)]
    slot_back(0)
    prepare(0)
    r_x1 = [give_back(gk, rgk, 0, 0, 8)]
    prepare(1)
    gathered = share_z(at_three, xsum2, zin2, zbuf2)
    back_k(3)
    backward(OWN, BLOCK, k_ref, v_ref, own_gk, own_gv)
    back_v(3)
    gathered()
    xg = gather_x(zbuf2, agx2)
    agx2[my_x] = zbuf2[...]
    back_k(2)
    back_v(2)
    dq_ref[...] = (dqt[...] * SCALE).T.astype(BF16)
    wait_recv(xg)
    sg_k = agx2[0:2].reshape(SUM, DIM)
    sg_v = agx2[2:4].reshape(SUM, DIM)
    term = dot_nt(sg_k, k_ref[...]) + dot_nt(sg_v, v_ref[...])
    term = term.astype(BF16).reshape(4, 2, 2, 16, BLOCK)
    t_ref[:, 0] = term[:, :, 0]
    t_ref[:, 1] = term[:, :, 1]

    def exchange(hi, into):
        return [
            copy(
                t_ref.at[lax.div(flipped(head, m), 4), lax.rem(flipped(head, m), 2), hi], into.at[j], "head", m
            )
            for j, m in enumerate(HEAD_MASKS)
        ]

    def summed(hi, arrived):
        total = t_ref[my_y, my_core, hi].astype(F32)
        for j in range(7):
            total = total + arrived[j].astype(F32)
        return total

    first = exchange(1 - my_hi, rt)
    second = exchange(my_hi, rt2)
    r_x2.append(give_back(gv, rgv, 1, 2, 16))
    r_x1.append(give_back(gv, rgv, 0, 0, 8))
    own_gk[...] = own_gk[...] * SCALE + dot_tn(proj_ref[...], sg_k)
    own_gv[...] = own_gv[...] + dot_tn(proj_ref[...], sg_v)
    wait_recv(first)
    wb[...] = summed(1 - my_hi, rt).astype(BF16)

    @pl.when(my_z != 0)
    def _():
        pl.semaphore_wait(hi_sem, 1)

    hs = copy(wb, rh, "head", 2)
    back_k(1)
    back_v(1)
    wait_recv(second)
    w_ref[...] = summed(my_hi, rt2)
    for c, j in ((r_x1, 0), (r_x2, 1)):
        wait_recv(c)
        own_gk[...] += rgk[j].astype(F32)
        own_gv[...] += rgv[j].astype(F32)
    up_arrives, down_arrives = my_z > 0, my_z < 7
    for back, own, into, result in ((back_k, own_gk, zrk, dk_ref), (back_v, own_gv, zrv, dv_ref)):
        back(0)
        result[...] = (
            own[...]
            + jnp.where(up_arrives, into[0, 0].astype(F32), 0.0)
            + jnp.where(down_arrives, into[1, 0].astype(F32), 0.0)
        ).astype(BF16)
    hs.wait_recv()
    dproj_ref[...] = w_ref[...] + rh[...].astype(F32)
    for c in sent:
        c.wait_send()
    for end in closing:
        end()


def put_out(*refs):
    sem = refs[-1]
    copies = [pltpu.make_async_copy(refs[i], refs[5 + i], sem.at[i]) for i in range(5)]
    for c in copies:
        c.start()
    for c in copies:
        c.wait()


def per_device(queries, key_tokens, value_tokens, output_gradient, summary_proj, partner_bits):
    vmem = pl.BlockSpec(memory_space=pltpu.VMEM)
    smem = pl.BlockSpec(memory_space=pltpu.SMEM)
    V = pltpu.VMEM
    out, dq, dk, dv, dproj = pl.pallas_call(
        kernel,
        name="butterfly",
        out_shape=(
            pltpu.VMEM((ROWS, DIM), BF16),
            pltpu.VMEM((ROWS, DIM), BF16),
            pltpu.VMEM((BLOCK, DIM), BF16),
            pltpu.VMEM((BLOCK, DIM), BF16),
            pltpu.VMEM((16, BLOCK), F32),
        ),
        in_specs=[smem] + [pl.BlockSpec(memory_space=pl.ANY)] * 5,
        out_specs=[vmem] * 5,
        scratch_shapes=[
            V((ROWS, DIM), BF16), V((BLOCK, DIM), BF16), V((BLOCK, DIM), BF16),
            V((ROWS, DIM), BF16), V((SUM, BLOCK), BF16), pltpu.SemaphoreType.DMA((5,)),
            V((DIM, ROWS), BF16), V((DIM, ROWS), BF16),
            V((4, 2, 64, DIM), F32), V((3, 2, 64, DIM), F32),
            V((2, 64, DIM), F32), V((7, 64, DIM), BF16),
            V((2, 64, DIM), BF16), V((2, 64, DIM), BF16), V((4, 2, 64, DIM), BF16),
            V((2, BLOCK, DIM), BF16), V((2, BLOCK, DIM), BF16),
            V((2, 4, BLOCK, DIM), BF16), V((2, 4, BLOCK, DIM), BF16),
            V((5, BLOCK, DIM), BF16), V((5, BLOCK, DIM), BF16),
            V((5 * BLOCK + SUM, ROWS), BF16),
            V((1, ROWS), F32), V((1, ROWS), F32), V((8, ROWS), F32),
            V((1, ROWS), F32), V((1, ROWS), F32),
            V((DIM, ROWS), F32), V((DIM, ROWS), F32),
            V((BLOCK, DIM), F32), V((BLOCK, DIM), F32),
            V((BLOCK, DIM), F32), V((BLOCK, DIM), F32),
            V((4, BLOCK, DIM), BF16), V((4, BLOCK, DIM), BF16),
            V((5, BLOCK, DIM), BF16), V((5, BLOCK, DIM), BF16),
            V((2, BLOCK, DIM), BF16), V((2, BLOCK, DIM), BF16),
            V((2, 2, BLOCK, DIM), BF16), V((2, 2, BLOCK, DIM), BF16),
            V((2, 4, BLOCK, DIM), BF16), V((2, 4, BLOCK, DIM), BF16),
            V((4, 2, 64, DIM), BF16), V((3, 2, 64, DIM), BF16),
            V((2, 64, DIM), F32), V((7, 64, DIM), BF16),
            V((2, 64, DIM), BF16), V((2, 64, DIM), BF16), V((4, 2, 64, DIM), BF16),
            V((4, 2, 2, 16, BLOCK), BF16), V((7, 16, BLOCK), BF16), V((7, 16, BLOCK), BF16),
            V((16, BLOCK), F32), V((16, BLOCK), BF16), V((16, BLOCK), BF16),
            pltpu.SemaphoreType.DMA((COPIES,)), pltpu.SemaphoreType.DMA((COPIES,)),
            pltpu.SemaphoreType.REGULAR((6,)), pltpu.SemaphoreType.REGULAR, pltpu.SemaphoreType.REGULAR,
        ],
        compiler_params=pltpu.CompilerParams(
            collective_id=0, has_side_effects=True, vmem_limit_bytes=60 * 1024 * 1024
        ),
    )(
        partner_bits,
        queries.reshape(ROWS, DIM),
        key_tokens.reshape(BLOCK, DIM),
        value_tokens.reshape(BLOCK, DIM),
        output_gradient.reshape(ROWS, DIM),
        summary_proj,
    )
    anywhere = pl.BlockSpec(memory_space=pl.ANY)
    held = (out, dq, dk, dv, dproj)
    held = tuple(pltpu.with_memory_space_constraint(a, pltpu.VMEM) for a in held)
    out, dq, dk, dv, dproj = pl.pallas_call(
        put_out,
        name="put_out",
        out_shape=tuple(jax.ShapeDtypeStruct(a.shape, a.dtype) for a in held),
        in_specs=[vmem] * 5,
        out_specs=[anywhere] * 5,
        scratch_shapes=[pltpu.SemaphoreType.DMA((5,))],
    )(*held)
    return (
        out.reshape(queries.shape),
        dq.reshape(queries.shape),
        dk.reshape(key_tokens.shape),
        dv.reshape(value_tokens.shape),
        dproj,
    )


def solution(mesh):
    rows = P("head", "seq", None)
    return jax.shard_map(
        per_device,
        mesh=mesh,
        in_specs=(rows, rows, rows, rows, P(None, "seq"), P("seq", None)),
        out_specs=(rows, rows, rows, rows, P("head", "seq")),
        check_vma=False,
    )
```

```python
import functools
import math

import jax
import jax.numpy as jnp
from jax import lax
from jax.experimental import pallas as pl
from jax.experimental.pallas import tpu as pltpu
from jax.sharding import PartitionSpec as P

MESH = pl.DeviceIdType.MESH
BLOCK = 512
DIM = 128
ROWS = 1024
SUM = 256
CHUNK = 512
SCALE = 1.0 / 12.0
COPIES = 120
EXP2_SCALE = math.log2(math.e) / 12.0
F32, BF16 = jnp.float32, jnp.bfloat16

LAST = {0: 4, 1: 5, 2: 6, 3: 7, 4: 6, 5: 7, 6: 7}
RELAY_IN = {s: [z for z in range(s, 8) if LAST[z - s] >= z] for s in (1, 2, 3, 4)}
RELAY_OUT = {s: [z - 1 for z in RELAY_IN[s]] for s in (1, 2, 3, 4)}

ORDER = (3, 0, 4, 1, 2)
Z_MASKS = tuple(range(1, 8))
X_MASKS = (8, 16, 24)
HEAD_MASKS = (1, 4, 5, 8, 9, 12, 13)

OWN, SLOT, SUMMARY = 0, 1, 5


def flipped(index, mask):
    out = index
    bit = 1
    while bit <= mask:
        if mask & bit:
            out = out + bit * (1 - 2 * lax.rem(lax.div(index, bit), 2))
        bit *= 2
    return out


def dot(a, b):
    return lax.dot_general(a, b, (((1,), (0,)), ((), ())), preferred_element_type=F32)


def dot_nt(a, b):
    return lax.dot_general(a, b, (((1,), (1,)), ((), ())), preferred_element_type=F32)


def dot_tn(a, b):
    return lax.dot_general(a, b, (((0,), (0,)), ((), ())), preferred_element_type=F32)


def kernel(
    bits_ref, q_in, k_in, v_in, do_in, proj_in,
    out_ref, dq_ref, dk_ref, dv_ref, dproj_ref,
    q_ref, k_ref, v_ref, do_ref, proj_ref, load_sem,
    qt, dot_t, part, rx, xsum, zin, zbuf, agx,
    kx, vx, kz, vz, ks, vs, e_ref, m_ref, l_ref, mslot, rescale, delta_ref, acc, dqt,
    gka, gva, own_gk, own_gv, gslot_k, gslot_v, gk, gv, rgk, rgv, zsk, zsv, zrk, zrv,
    part2, rx2, xsum2, zin2, half2, zbuf2, agx2,
    t_ref, rt, rt2, w_ref, wb, rh,
    send_sem, recv_sem, near_sem, edge_sem, hi_sem,
):
    seq = lax.axis_index("seq")
    head = lax.axis_index("head")
    my_x, my_z = lax.div(seq, 8), lax.rem(seq, 8)
    my_y, my_hi, my_core = lax.div(head, 4), lax.rem(lax.div(head, 2), 2), lax.rem(head, 2)
    middle = (my_z == 3) | (my_z == 4)

    barrier = pltpu.get_barrier_semaphore()

    def greet(device):
        pl.semaphore_signal(barrier, inc=1, device_id=device, device_id_type=MESH)

    for mask in X_MASKS:
        greet({"seq": flipped(seq, mask)})
    for mask in HEAD_MASKS:
        greet({"head": flipped(head, mask)})

    @pl.when(my_z < 7)
    def _():
        greet({"seq": seq + 1})

    @pl.when(my_z > 0)
    def _():
        greet({"seq": seq - 1})

    @pl.when(my_z == 0)
    def _():
        greet({"seq": seq + 7, "head": flipped(head, 2)})

    @pl.when(my_z == 7)
    def _():
        greet({"seq": seq - 7, "head": flipped(head, 2)})

    loads = [
        pltpu.make_async_copy(src, dst, load_sem.at[n])
        for n, (src, dst) in enumerate(
            ((k_in, k_ref), (v_in, v_ref), (proj_in, proj_ref), (q_in, q_ref), (do_in, do_ref))
        )
    ]
    for load in loads:
        load.start()

    def one_of(places, mirrored=False):
        found = None
        for z in places:
            here = my_z == (7 - z if mirrored else z)
            found = here if found is None else found | here
        return found

    closing = []
    ids = iter(range(COPIES))
    sent = []

    def start(c):
        c.start()
        sent.append(c)
        return c

    def describe(src, dst, device, n, m):
        return pltpu.make_async_remote_copy(
            src_ref=src, dst_ref=dst, send_sem=send_sem.at[n], recv_sem=recv_sem.at[m],
            device_id=device, device_id_type=MESH,
        )

    def copy(src, dst, axis, mask):
        n = next(ids)
        return start(describe(src, dst, {axis: flipped(seq if axis == "seq" else head, mask)}, n, n))

    def wait_recv(cs):
        for c in cs:
            c.wait_recv()

    for load in loads[:3]:
        load.wait()

    proj = proj_ref[...]
    part[0:2] = dot(proj, k_ref[...]).reshape(2, 2, 64, DIM)
    part[2:4] = dot(proj, v_ref[...]).reshape(2, 2, 64, DIM)
    for load in loads[3:]:
        load.wait()
    qt[...] = q_ref[...].T
    dot_t[...] = do_ref[...].T

    missing = 10 - (bits_ref[0, 0] + bits_ref[0, 1] + bits_ref[0, 2] + bits_ref[0, 3])
    place = jnp.int32(0)
    for i, b in enumerate(ORDER):
        place = place + jnp.where(missing == b, i, 0)

    pl.semaphore_wait(barrier, 2 + len(X_MASKS) + len(HEAD_MASKS))

    def tell(n):
        for way, there in ((0, my_z < 7), (1, my_z > 0)):
            @pl.when(there)
            def _():
                pl.semaphore_signal(
                    near_sem.at[2 * n + way], inc=1, device_id={"seq": seq + 1 - 2 * way}, device_id_type=MESH
                )

    def hear(n):
        for way, there in ((0, my_z > 0), (1, my_z < 7)):
            @pl.when(there)
            def _():
                pl.semaphore_wait(near_sem.at[2 * n + way], 1)

    def fetch(j, mask):
        return (
            copy(k_ref, kx.at[j], "seq", mask),
            copy(v_ref, vx.at[j], "seq", mask),
        )

    def relay(source, into, n):
        pieces = []
        for way in (0, 1):
            i = next(ids)
            device = {"seq": seq + 1 - 2 * way}
            pieces.append((way, i, device))

        def c(way, i, device):
            return describe(source(way), into(way), device, i, i)

        def go(senders):
            for way, i, device in pieces:
                @pl.when(one_of(senders, way == 1))
                def _():
                    c(way, i, device).start()

            def end():
                for way, i, device in pieces:
                    @pl.when(one_of(senders, way == 1))
                    def _():
                        c(way, i, device).wait_send()

            closing.append(end)

        def arrived(receivers):
            for way, i, device in pieces:
                @pl.when(one_of(receivers, way == 1))
                def _():
                    c(way, i, device).wait_recv()

        return go, arrived

    def fetch_z(own, into):
        steps = []
        for n in (1, 2, 3, 4):
            source = (lambda way: own) if n == 1 else (lambda way, n=n: into.at[way, n - 2])
            steps.append(relay(source, lambda way, n=n: into.at[way, n - 1], n))

        def go(n):
            if n > 1:
                steps[n - 2][1](RELAY_IN[n - 1])
            if n <= 4:
                steps[n - 1][0](RELAY_OUT[n])

        return go

    def scatter_x(src, dst):
        return [
            copy(src.at[lax.div(flipped(seq, m), 8)], dst.at[j], "seq", m)
            for j, m in enumerate(X_MASKS)
        ]

    def gather_x(src, dst):
        return [copy(src, dst.at[my_x], "seq", m) for m in X_MASKS]

    def reduce_z(halves, into):
        sends = [next(ids) for _ in range(2)]
        first = [next(ids) for _ in range(7)][0]
        for r in range(2):
            apart = flipped(my_z, 3 + r)

            @pl.when(my_z != 3 + r)
            def _():
                describe(
                    halves.at[r], into.at[apart - 1], {"seq": seq - my_z + (3 + r)}, sends[r], first + apart - 1
                ).start()

        def end():
            for r in range(2):
                @pl.when(my_z != 3 + r)
                def _():
                    describe(halves.at[r], into.at[0], {"seq": flipped(seq, 1)}, sends[r], first).wait_send()

        closing.append(end)
        return first

    def share_z(first, sums, into, buf):
        sends = [next(ids) for _ in range(7)]
        arrive = [next(ids) for _ in range(2)]

        @pl.when(middle)
        def _():
            r = my_z - 3
            total = sums[r]
            for j in range(7):
                describe(into.at[j], into.at[j], {"seq": flipped(seq, 1)}, sends[0], first + j).wait_recv()
                total = total + into[j].astype(F32)
            buf[r] = total.astype(BF16)
            for j, m in enumerate(Z_MASKS):
                describe(buf.at[r], buf.at[r], {"seq": flipped(seq, m)}, sends[j], arrive[0] + r).start()

        def arrived():
            for r in range(2):
                @pl.when(my_z != 3 + r)
                def _():
                    describe(buf.at[r], buf.at[r], {"seq": flipped(seq, 1)}, sends[0], arrive[r]).wait_recv()

        def end():
            @pl.when(middle)
            def _():
                for j in range(7):
                    describe(buf.at[0], buf.at[0], {"seq": flipped(seq, 1)}, sends[j], arrive[0]).wait_send()

        closing.append(end)
        return arrived

    def scores(row, n, k, first=False):
        base = row * BLOCK

        def step(c, carry):
            cols = pl.ds(pl.multiple_of(c * CHUNK, CHUNK), CHUNK)
            s = dot(k[...], qt[:, cols])
            top = jnp.max(s, axis=0, keepdims=True)
            if not first:
                before = m_ref[:, cols]
                top = jnp.maximum(before, top)
                alpha = jnp.exp2((before - top) * EXP2_SCALE)
                rescale[:, cols] = alpha
            e = jnp.exp2((s - top) * EXP2_SCALE)
            total = jnp.sum(e, axis=0, keepdims=True)
            e_ref[base : base + n, cols] = e.astype(BF16)
            if not first:
                total = l_ref[:, cols] * alpha + total
            l_ref[:, cols] = total
            m_ref[:, cols] = top
            mslot[row : row + 1, cols] = top
            return carry

        lax.fori_loop(0, ROWS // CHUNK, step, 0)

    def mix(row, n, v, first=False):
        base = row * BLOCK

        def step(c, carry):
            cols = pl.ds(pl.multiple_of(c * CHUNK, CHUNK), CHUNK)
            mixed = dot_tn(v[...], e_ref[base : base + n, cols])
            if not first:
                mixed = acc[:, cols] * rescale[:, cols] + mixed
            acc[:, cols] = mixed
            return carry

        lax.fori_loop(0, ROWS // CHUNK, step, 0)

    def forward(row, n, k, v, first=False):
        scores(row, n, k, first)
        mix(row, n, v, first)

    from_above = [1 - lax.rem(lax.div(my_z, b), 2) for b in (1, 2, 4)]

    def partner(i, x, z):
        if ORDER[i] >= 3:
            return x[ORDER[i] - 3]
        bit = ORDER[i]
        return z[from_above[bit], (1 << bit) - 1]

    def choose(i, chosen, x, z):
        chosen[i] = jnp.where(i < place, partner(i, x, z), partner(i + 1, x, z))

    go_k, go_v = fetch_z(k_ref, kz), fetch_z(v_ref, vz)
    go_k(1)
    go_v(1)
    tell(0)
    xs = scatter_x(part, rx)
    f_x1 = fetch(0, 8)
    f_x2 = fetch(1, 16)
    forward(OWN, BLOCK, k_ref, v_ref, first=True)
    hear(0)
    tell(1)
    go_k(2)
    hear(1)
    tell(2)
    wait_recv(xs)
    xsum[...] = part[my_x] + rx[0] + rx[1] + rx[2]
    hear(2)
    at_three = reduce_z(xsum, zin)
    go_v(2)
    wait_recv(f_x1)
    choose(0, ks, kx, kz)
    choose(0, vs, vx, vz)
    forward(SLOT, BLOCK, ks.at[0], vs.at[0])
    go_k(3)
    gathered = share_z(at_three, xsum, zin, zbuf)
    go_v(3)
    wait_recv(f_x2)
    choose(1, ks, kx, kz)
    choose(1, vs, vx, vz)
    forward(SLOT + 1, BLOCK, ks.at[1], vs.at[1])
    go_k(4)
    gathered()
    xg = gather_x(zbuf, agx)
    agx[my_x] = zbuf[...]
    go_v(4)
    choose(2, ks, kx, kz)
    choose(2, vs, vx, vz)
    forward(SLOT + 2, BLOCK, ks.at[2], vs.at[2])

    @pl.when(my_z == 7)
    def _():
        pl.semaphore_signal(
            edge_sem, inc=1, device_id={"seq": seq - 7, "head": flipped(head, 2)}, device_id_type=MESH
        )

    dqt[...] = jnp.zeros_like(dqt)
    wait_recv(xg)
    sk, sv = ks.at[4, 0:SUM], vs.at[4, 0:SUM]
    sk[...] = agx[0:2].reshape(SUM, DIM)
    sv[...] = agx[2:4].reshape(SUM, DIM)
    forward(SUMMARY, SUM, sk, sv)

    go_k(5)
    choose(3, ks, kx, kz)
    scores(SLOT + 3, BLOCK, ks.at[3])
    l_ref[...] = 1.0 / l_ref[...]

    def weights(row, n, cols):
        base = row * BLOCK
        factor = jnp.exp2((mslot[row : row + 1, cols] - m_ref[:, cols]) * EXP2_SCALE) * l_ref[:, cols]
        return e_ref[base : base + n, cols].astype(F32) * factor

    summary_gv = jnp.zeros((SUM, DIM), F32)
    for c in range(ROWS // CHUNK):
        cols = pl.ds(c * CHUNK, CHUNK)
        summary_gv = summary_gv + dot(weights(SUMMARY, SUM, cols).astype(BF16), do_ref[cols, :])
    part2[2:4] = summary_gv.astype(BF16).reshape(2, 2, 64, DIM)
    x_ids = [next(ids) for _ in X_MASKS]

    def part_to(j):
        peer = flipped(seq, X_MASKS[j])
        return describe(part2.at[lax.div(peer, 8)], rx2.at[j], {"seq": peer}, x_ids[j], x_ids[j])

    def send_parts(values):
        for j, m in enumerate(X_MASKS):
            peer_x = lax.div(flipped(seq, m), 8)

            @pl.when((peer_x >= 2) if values else (peer_x < 2))
            def _():
                part_to(j).start()

    send_parts(True)
    go_v(5)
    choose(3, vs, vx, vz)
    mix(SLOT + 3, BLOCK, vs.at[3])

    attended = acc[...] * l_ref[...]
    delta_ref[...] = jnp.sum(attended * dot_t[...].astype(F32), axis=0, keepdims=True)

    def backward(row, n, k, v, gk_acc, gv_acc):
        gk_acc[...] = jnp.zeros_like(gk_acc)
        if gv_acc is not None:
            gv_acc[...] = jnp.zeros_like(gv_acc)

        def step(c, carry):
            cols = pl.ds(pl.multiple_of(c * CHUNK, CHUNK), CHUNK)
            p = weights(row, n, cols)
            dp = dot(v[...], dot_t[:, cols])
            ds = (p * (dp - delta_ref[:, cols])).astype(BF16)
            dqt[:, cols] += dot_tn(k[...], ds)
            gk_acc[...] += dot(ds, q_ref[cols, :])
            if gv_acc is not None:
                gv_acc[...] += dot(p.astype(BF16), do_ref[cols, :])
            return carry

        lax.fori_loop(0, ROWS // CHUNK, step, 0)

    half_k = gka.at[0:SUM]
    backward(SUMMARY, SUM, sk, sv, half_k, None)
    part2[0:2] = (half_k[...] * SCALE).astype(BF16).reshape(2, 2, 64, DIM)
    send_parts(False)
    xs = [part_to(j) for j in range(3)]
    sent.extend(xs)

    def slot_back(i):
        backward(SLOT + i, BLOCK, ks.at[i], vs.at[i], gka, gva)
        gslot_k[i] = (gka[...] * SCALE).astype(BF16)
        gslot_v[i] = gva[...].astype(BF16)

    def prepare(i):
        for slots, g in ((gslot_k, gk), (gslot_v, gv)):
            zero = jnp.zeros((BLOCK, DIM), BF16)
            early = slots[i] if i < 4 else zero
            late = slots[i - 1] if i > 0 else zero
            g[i] = jnp.where(i < place, early, jnp.where(i > place, late, zero))

    def give_back(g, into, j, i, mask):
        return copy(g.at[i], into.at[j], "seq", mask)

    def return_z(g, sums, into):
        steps = {}
        for n in (4, 3, 2, 1):
            if n == 4:
                source = lambda way: g.at[4]
            elif n == 3:
                source = lambda way: into.at[way, 3]
            else:
                source = lambda way, n=n: sums.at[way, n - 1]
            steps[n] = relay(source, lambda way, n=n: into.at[way, n - 1], n)

        def up_down(places):
            return [7 - z for z in places]

        def go(n):
            if n < 4:
                steps[n + 1][1](up_down(RELAY_OUT[n + 1]))
            if n in (1, 2):
                own_value = g[3 if n == 2 else 1].astype(F32)
                for way in (0, 1):
                    came = one_of(up_down(RELAY_OUT[n + 1]), way == 1)
                    mine = from_above[n - 1] == 1 - way
                    sums[way, n - 1] = (
                        jnp.where(came, into[way, n].astype(F32), 0.0) + jnp.where(mine, own_value, 0.0)
                    ).astype(BF16)
            if n > 0:
                steps[n][0](up_down(RELAY_IN[n]))

        return go

    back_k, back_v = return_z(gk, zsk, zrk), return_z(gv, zsv, zrv)
    out_ref[...] = (acc[...] * l_ref[...]).T.astype(BF16)
    slot_back(3)
    prepare(4)
    wait_recv(xs)
    xsum2[...] = (
        part2[my_x].astype(F32) + rx2[0].astype(F32) + rx2[1].astype(F32) + rx2[2].astype(F32)
    )
    half2[...] = xsum2[...].astype(BF16)
    at_three = reduce_z(half2, zin2)
    back_k(4)
    back_v(4)
    slot_back(2)
    prepare(3)
    slot_back(1)
    prepare(2)
    r_x2 = [give_back(gk, rgk, 1, 2, 16)]
    slot_back(0)
    prepare(0)
    r_x1 = [give_back(gk, rgk, 0, 0, 8)]
    prepare(1)
    gathered = share_z(at_three, xsum2, zin2, zbuf2)

    @pl.when(my_z == 0)
    def _():
        pl.semaphore_wait(edge_sem, 1)
        for m in Z_MASKS:
            pl.semaphore_signal(hi_sem, inc=1, device_id={"seq": seq + m}, device_id_type=MESH)

    back_k(3)
    backward(OWN, BLOCK, k_ref, v_ref, own_gk, own_gv)
    back_v(3)
    gathered()
    xg = gather_x(zbuf2, agx2)
    agx2[my_x] = zbuf2[...]
    back_k(2)
    back_v(2)
    dq_ref[...] = (dqt[...] * SCALE).T.astype(BF16)
    wait_recv(xg)
    sg_k = agx2[0:2].reshape(SUM, DIM)
    sg_v = agx2[2:4].reshape(SUM, DIM)
    term = dot_nt(sg_k, k_ref[...]) + dot_nt(sg_v, v_ref[...])
    term = term.astype(BF16).reshape(4, 2, 2, 16, BLOCK)
    t_ref[:, 0] = term[:, :, 0]
    t_ref[:, 1] = term[:, :, 1]

    def exchange(hi, into):
        return [
            copy(
                t_ref.at[lax.div(flipped(head, m), 4), lax.rem(flipped(head, m), 2), hi], into.at[j], "head", m
            )
            for j, m in enumerate(HEAD_MASKS)
        ]

    def summed(hi, arrived):
        total = t_ref[my_y, my_core, hi].astype(F32)
        for j in range(7):
            total = total + arrived[j].astype(F32)
        return total

    first = exchange(1 - my_hi, rt)
    second = exchange(my_hi, rt2)
    r_x2.append(give_back(gv, rgv, 1, 2, 16))
    r_x1.append(give_back(gv, rgv, 0, 0, 8))
    own_gk[...] = own_gk[...] * SCALE + dot_tn(proj_ref[...], sg_k)
    own_gv[...] = own_gv[...] + dot_tn(proj_ref[...], sg_v)
    wait_recv(first)
    wb[...] = summed(1 - my_hi, rt).astype(BF16)

    @pl.when(my_z != 0)
    def _():
        pl.semaphore_wait(hi_sem, 1)

    hs = copy(wb, rh, "head", 2)
    back_k(1)
    back_v(1)
    wait_recv(second)
    w_ref[...] = summed(my_hi, rt2)
    for c, j in ((r_x1, 0), (r_x2, 1)):
        wait_recv(c)
        own_gk[...] += rgk[j].astype(F32)
        own_gv[...] += rgv[j].astype(F32)
    up_arrives, down_arrives = my_z > 0, my_z < 7
    for back, own, into, result in ((back_k, own_gk, zrk, dk_ref), (back_v, own_gv, zrv, dv_ref)):
        back(0)
        result[...] = (
            own[...]
            + jnp.where(up_arrives, into[0, 0].astype(F32), 0.0)
            + jnp.where(down_arrives, into[1, 0].astype(F32), 0.0)
        ).astype(BF16)
    hs.wait_recv()
    dproj_ref[...] = w_ref[...] + rh[...].astype(F32)
    for c in sent:
        c.wait_send()
    for end in closing:
        end()


def put_out(*refs):
    sem = refs[-1]
    copies = [pltpu.make_async_copy(refs[i], refs[5 + i], sem.at[i]) for i in range(5)]
    for c in copies:
        c.start()
    for c in copies:
        c.wait()


def per_device(queries, key_tokens, value_tokens, output_gradient, summary_proj, partner_bits):
    vmem = pl.BlockSpec(memory_space=pltpu.VMEM)
    smem = pl.BlockSpec(memory_space=pltpu.SMEM)
    V = pltpu.VMEM
    out, dq, dk, dv, dproj = pl.pallas_call(
        kernel,
        name="butterfly",
        out_shape=(
            pltpu.VMEM((ROWS, DIM), BF16),
            pltpu.VMEM((ROWS, DIM), BF16),
            pltpu.VMEM((BLOCK, DIM), BF16),
            pltpu.VMEM((BLOCK, DIM), BF16),
            pltpu.VMEM((16, BLOCK), F32),
        ),
        in_specs=[smem] + [pl.BlockSpec(memory_space=pl.ANY)] * 5,
        out_specs=[vmem] * 5,
        scratch_shapes=[
            V((ROWS, DIM), BF16), V((BLOCK, DIM), BF16), V((BLOCK, DIM), BF16),
            V((ROWS, DIM), BF16), V((SUM, BLOCK), BF16), pltpu.SemaphoreType.DMA((5,)),
            V((DIM, ROWS), BF16), V((DIM, ROWS), BF16),
            V((4, 2, 64, DIM), F32), V((3, 2, 64, DIM), F32),
            V((2, 64, DIM), F32), V((7, 64, DIM), F32),
            V((2, 64, DIM), BF16), V((4, 2, 64, DIM), BF16),
            V((2, BLOCK, DIM), BF16), V((2, BLOCK, DIM), BF16),
            V((2, 4, BLOCK, DIM), BF16), V((2, 4, BLOCK, DIM), BF16),
            V((5, BLOCK, DIM), BF16), V((5, BLOCK, DIM), BF16),
            V((5 * BLOCK + SUM, ROWS), BF16),
            V((1, ROWS), F32), V((1, ROWS), F32), V((8, ROWS), F32),
            V((1, ROWS), F32), V((1, ROWS), F32),
            V((DIM, ROWS), F32), V((DIM, ROWS), F32),
            V((BLOCK, DIM), F32), V((BLOCK, DIM), F32),
            V((BLOCK, DIM), F32), V((BLOCK, DIM), F32),
            V((4, BLOCK, DIM), BF16), V((4, BLOCK, DIM), BF16),
            V((5, BLOCK, DIM), BF16), V((5, BLOCK, DIM), BF16),
            V((2, BLOCK, DIM), BF16), V((2, BLOCK, DIM), BF16),
            V((2, 2, BLOCK, DIM), BF16), V((2, 2, BLOCK, DIM), BF16),
            V((2, 4, BLOCK, DIM), BF16), V((2, 4, BLOCK, DIM), BF16),
            V((4, 2, 64, DIM), BF16), V((3, 2, 64, DIM), BF16),
            V((2, 64, DIM), F32), V((7, 64, DIM), BF16),
            V((2, 64, DIM), BF16), V((2, 64, DIM), BF16), V((4, 2, 64, DIM), BF16),
            V((4, 2, 2, 16, BLOCK), BF16), V((7, 16, BLOCK), BF16), V((7, 16, BLOCK), BF16),
            V((16, BLOCK), F32), V((16, BLOCK), BF16), V((16, BLOCK), BF16),
            pltpu.SemaphoreType.DMA((COPIES,)), pltpu.SemaphoreType.DMA((COPIES,)),
            pltpu.SemaphoreType.REGULAR((6,)), pltpu.SemaphoreType.REGULAR, pltpu.SemaphoreType.REGULAR,
        ],
        compiler_params=pltpu.CompilerParams(
            collective_id=0, has_side_effects=True, vmem_limit_bytes=60 * 1024 * 1024
        ),
    )(
        partner_bits,
        queries.reshape(ROWS, DIM),
        key_tokens.reshape(BLOCK, DIM),
        value_tokens.reshape(BLOCK, DIM),
        output_gradient.reshape(ROWS, DIM),
        summary_proj,
    )
    anywhere = pl.BlockSpec(memory_space=pl.ANY)
    held = (out, dq, dk, dv, dproj)
    held = tuple(pltpu.with_memory_space_constraint(a, pltpu.VMEM) for a in held)
    out, dq, dk, dv, dproj = pl.pallas_call(
        put_out,
        name="put_out",
        out_shape=tuple(jax.ShapeDtypeStruct(a.shape, a.dtype) for a in held),
        in_specs=[vmem] * 5,
        out_specs=[anywhere] * 5,
        scratch_shapes=[pltpu.SemaphoreType.DMA((5,))],
    )(*held)
    return (
        out.reshape(queries.shape),
        dq.reshape(queries.shape),
        dk.reshape(key_tokens.shape),
        dv.reshape(value_tokens.shape),
        dproj,
    )


def solution(mesh):
    rows = P("head", "seq", None)
    return jax.shard_map(
        per_device,
        mesh=mesh,
        in_specs=(rows, rows, rows, rows, P(None, "seq"), P("seq", None)),
        out_specs=(rows, rows, rows, rows, P("head", "seq")),
        check_vma=False,
    )
```
